32 devices in a mesh: groups: 2 (over x), head: 8 (over z, y), tensor: 2 (over core).
Axes of the slice: x: 2, y: 2, z: 4, core: 2. Of those that a mesh axis runs over, the one named last changes fastest.
Arguments:
- query: bfloat16 [8192, 1024], P(('groups', 'head'), 'tensor'), parts along dimension 0, may hold values from -32 to 32
- keys_in: bfloat16 [8192, 1024], P(('groups', 'head'), 'tensor'), parts along dimension 0, may hold values from -6 to 6
- values_in: bfloat16 [8192, 1024], P(('groups', 'head'), 'tensor'), parts along dimension 0, may hold values from -6 to 6
- grad_out: bfloat16 [8192, 1024], P(('groups', 'head'), 'tensor'), parts along dimension 0, may hold values from -96 to 96
- w_out: bfloat16 [1024, 1024], P('tensor'), may hold values from -0.1875 to 0.1875
- w_query: bfloat16 [1024, 1024], P(None, 'tensor'), may hold values from -0.1875 to 0.1875
- w_key: bfloat16 [1024, 1024], P(None, 'tensor'), may hold values from -0.1875 to 0.1875
- w_value: bfloat16 [1024, 1024], P(None, 'tensor'), may hold values from -0.1875 to 0.1875
- perm: int32 [2, 4096], P('groups'), parts along dimension 0, may hold values from 0 to 4095, as said below
- blocks: int32 [2, 32, 12], P('groups'), parts along dimension 0, may hold values from 0 to 31, as said below
- counts: int32 [2, 32], P('groups'), parts along dimension 0, may hold values from 1 to 12
Outputs:
- input_grad: bfloat16 [8192, 1024], P(('groups', 'head', 'tensor')), parts along dimension 0
The draws below stay inside these ranges and needn't reach their ends.
There are 2 independent parts, one for each index of `groups`. The reference program is written for one: setup_inputs(seed, part) draws one part's arguments, and reference() takes and returns one part's arrays. A program takes and returns all parts, laid end to end along the dimension named above; an argument that names none is the same for every part. Nothing has to cross between parts.
Inputs may be any that keep to these rules, and one draw needn't show every extreme that they name: Each row of perm holds every node number of the graph once. blocks[g, b, 0] is b; the 12 entries of blocks[g, b] are different block numbers.
All inputs are finite; a program needn't handle non-finite values.
Results may differ from the reference program's by a relative error of at most 0.011.
Values may be sent and summed in bfloat16 or wider, within the bound.
A program may use at most 64 MiB of HBM per device.

```python
import jax
import jax.numpy as jnp
from jax import lax

H = 16
HD = 64
D = 1024
BS = 128
KB = 12
PARTITIONS = 8
G = 1
R = 512
NG = 4096
NB = 32
NODES = 4096


def order_of(key):
    scores = jax.random.randint(jax.random.fold_in(key, 31), (G, NG), 0, 2 ** 16) * NG
    scores = scores + jnp.arange(NG, dtype=jnp.int32)[None, :]
    return jnp.argsort(scores, axis=1, stable=True).astype(jnp.int32)


def node_rows(values, order):
    width = values.shape[-1]
    placed = jnp.take_along_axis(values, order[:, :, None], axis=1)
    return placed.reshape(G, PARTITIONS, R, width).transpose(1, 2, 0, 3).reshape(NODES, width)


def draw_perm(key, part):
    return order_of(key)


def draw_keys_in(key, part):
    values = jnp.clip(jax.random.normal(jax.random.fold_in(key, 41), (G, NG, D), jnp.float32), -6.0, 6.0)
    return node_rows(values, order_of(key)).astype(jnp.bfloat16)


def draw_query(key, part):
    values = jnp.clip(jax.random.normal(jax.random.fold_in(key, 43), (G, NG, D), jnp.float32), -6.0, 6.0)
    return node_rows(values, order_of(key)).astype(jnp.bfloat16)


def draw_blocks(key, part):
    scores = jax.random.randint(jax.random.fold_in(key, 61), (G, NB, NB - 1), 0, 2 ** 16) * (NB - 1)
    scores = scores + jnp.arange(NB - 1, dtype=jnp.int32)[None, None, :]
    shifts = jnp.argsort(scores, axis=2, stable=True)[:, :, :KB - 1].astype(jnp.int32) + 1
    offsets = jnp.concatenate((jnp.zeros((G, NB, 1), jnp.int32), shifts), axis=2)
    return ((jnp.arange(NB, dtype=jnp.int32)[None, :, None] + offsets) % NB).astype(jnp.int32)


def draw_counts(key, part):
    drawn = jax.random.randint(jax.random.fold_in(key, 67), (G, NB), 1, KB + 1).astype(jnp.int32)
    drawn = drawn.at[:, 0].set(KB)
    return drawn.at[:, 1].set(1)


def level_of(rng, shape, split, smallest, largest):
    def one(axis_at, blocks):
        steps = jax.random.uniform(jax.random.fold_in(jax.random.fold_in(rng, 6), axis_at), (blocks,), jnp.float32, smallest / len(split), largest / len(split))
        return jnp.repeat(jnp.exp(steps), shape[axis_at] // blocks).reshape((-1,) + (1,) * (len(shape) - axis_at - 1))

    loudness = one(*split[0])
    for cut in split[1:]:
        loudness = loudness * one(*cut)
    return loudness


def centred(stream_key, shape, scale, limit, pieces=(), held_as=jnp.bfloat16):
    loudness = level_of(stream_key, shape, pieces, -0.22, 0.18) if pieces else 1.0
    values = jax.random.normal(stream_key, shape, jnp.float32) * scale * loudness
    return jnp.minimum(jnp.maximum(values, -limit), limit).astype(held_as)


def setup_inputs(seed: int = 0, part: int = 0) -> dict:
    key_list = jax.random.split(jax.random.key(seed), 12)
    own_keys = jax.random.split(jax.random.fold_in(key_list[11], part), 12)
    query = draw_query(jax.random.fold_in(jax.random.fold_in(key_list[11], part), 71), part)
    keys_in = draw_keys_in(jax.random.fold_in(jax.random.fold_in(key_list[11], part), 71), part)
    values_in = centred(own_keys[2], (NODES, D), 1.0, 6.0, ((0, 8), (1, 2)))
    grad_out = centred(own_keys[3], (NODES, D), 16.0, 96.0, ((0, 8), (1, 2)))
    w_out = centred(key_list[4], (D, D), D ** -0.5, 0.1875, ((0, 2),))
    w_query = centred(key_list[5], (D, D), D ** -0.5, 0.1875, ((1, 2),))
    w_key = centred(key_list[6], (D, D), D ** -0.5, 0.1875, ((1, 2),))
    w_value = centred(key_list[7], (D, D), D ** -0.5, 0.1875, ((1, 2),))
    perm = draw_perm(jax.random.fold_in(jax.random.fold_in(key_list[11], part), 71), part)
    blocks = draw_blocks(jax.random.fold_in(jax.random.fold_in(key_list[11], part), 71), part)
    counts = draw_counts(jax.random.fold_in(jax.random.fold_in(key_list[11], part), 71), part)
    return dict(query=query, keys_in=keys_in, values_in=values_in, grad_out=grad_out, w_out=w_out, w_query=w_query, w_key=w_key, w_value=w_value, perm=perm, blocks=blocks, counts=counts)


def to_graphs(values):
    width = values.shape[-1]
    return values.reshape(PARTITIONS, R, G, width).transpose(2, 0, 1, 3).reshape(G, NG, width)


def to_rows(values):
    width = values.shape[-1]
    return values.reshape(G, PARTITIONS, R, width).transpose(1, 2, 0, 3).reshape(NODES, width)


def head_grads(query_head, keys_head, values_head, grads_head, listed, active):
    scale = HD ** -0.5
    query_blk = query_head.reshape(NB, BS, HD).astype(jnp.float32)
    grad_blk = grads_head.reshape(NB, BS, HD).astype(jnp.float32)
    key_blk = keys_head.reshape(NB, BS, HD).astype(jnp.float32)
    value_blk = values_head.reshape(NB, BS, HD).astype(jnp.float32)
    fetched_keys = key_blk[listed]
    fetched_values = value_blk[listed]
    score = jnp.einsum("qad,qjcd->qajc", query_blk, fetched_keys) * scale
    score = jnp.where(active[:, None, :, None], score, -jnp.inf)
    top = jnp.max(score, axis=(2, 3), keepdims=True)
    expo = jnp.exp(score - top)
    prob = expo / jnp.sum(expo, axis=(2, 3), keepdims=True)
    prob_b = lax.optimization_barrier(prob.astype(jnp.bfloat16)).astype(jnp.float32)
    attn = jnp.einsum("qajc,qjcd->qad", prob_b, fetched_values)
    delta = jnp.sum(grad_blk * attn, axis=-1)
    dprob = jnp.einsum("qad,qjcd->qajc", grad_blk, fetched_values)
    dscore = prob * (dprob - delta[:, :, None, None])
    dscore = lax.optimization_barrier(dscore.astype(jnp.bfloat16)).astype(jnp.float32)
    query_grad = jnp.einsum("qajc,qjcd->qad", dscore, fetched_keys) * scale
    key_terms = jnp.einsum("qajc,qad->qjcd", dscore, query_blk) * scale
    value_terms = jnp.einsum("qajc,qad->qjcd", prob_b, grad_blk)
    key_grad = jnp.zeros((NB, BS, HD), jnp.float32).at[listed].add(key_terms)
    value_grad = jnp.zeros((NB, BS, HD), jnp.float32).at[listed].add(value_terms)
    joined = jnp.concatenate((query_grad.reshape(NG, HD), key_grad.reshape(NG, HD), value_grad.reshape(NG, HD)), axis=1)
    return joined.astype(jnp.bfloat16)


def reference(query, keys_in, values_in, grad_out, w_out, w_query, w_key, w_value, perm, blocks, counts):
    attn_grad = jnp.dot(grad_out, w_out.T, preferred_element_type=jnp.float32).astype(jnp.bfloat16)
    stacked = jnp.stack([to_graphs(item) for item in (query, keys_in, values_in, attn_grad)], axis=1)

    def per_graph(inputs):
        member, order, listed, count_row = inputs
        inverse = jnp.zeros((NG,), jnp.int32).at[order].set(jnp.arange(NG, dtype=jnp.int32))
        by_node = jnp.take(member, inverse, axis=1)
        by_head = by_node.reshape(4, NG, H, HD).transpose(2, 0, 1, 3)
        active = jnp.arange(KB, dtype=jnp.int32)[None, :] < count_row[:, None]

        def per_head(parts):
            return head_grads(parts[0], parts[1], parts[2], parts[3], listed, active)

        grads = lax.map(per_head, by_head)
        grads = grads.reshape(H, NG, 3, HD).transpose(1, 2, 0, 3).reshape(NG, 3 * D)
        return jnp.take(grads, order, axis=0)

    per_part = lax.map(per_graph, (stacked, perm, blocks, counts))
    all_rows = to_rows(per_part)
    total = jnp.dot(all_rows[:, :D], w_query.T, preferred_element_type=jnp.float32)
    total = total + jnp.dot(all_rows[:, D:2 * D], w_key.T, preferred_element_type=jnp.float32)
    total = total + jnp.dot(all_rows[:, 2 * D:], w_value.T, preferred_element_type=jnp.float32)
    return total.astype(jnp.bfloat16)
```

```python
import jax
import jax.numpy as jnp
from jax import lax
from jax.experimental import pallas as pl
from jax.experimental.pallas import tpu as pltpu
from jax.sharding import PartitionSpec as P

HD = 64
BS = 128
NT = (((1,), (1,)), ((), ()))
UNROLL = 12
PACKED = 16
WIDE = 16
VMEM_BYTES = 67043328
MESH = pl.DeviceIdType.MESH


def dot(a, b):
    return jnp.dot(a, b, preferred_element_type=jnp.float32)


def marks(values, shape):
    return jnp.broadcast_to(values.astype(jnp.float32), shape).astype(jnp.bfloat16)


def hop(i, n):
    return n // 2 + (1 - 2 * lax.rem(i, 2)) * ((i + 1) // 2)


def spread(row_ref, q_hbm, k_hbm, v_hbm, go_hbm, w_hbm, qg_out, kv_out,
           q_ref, k_ref, v_ref, go_ref, w_ref, load_sem, grad_s, attn_s, kv_pack, qg_pack, kv_in, qg_in, acc_s, pair_sem, send_sem, recv_sem):
    n, part_rows, _ = kv_in.shape
    heads = q_ref.shape[1] // HD
    graphs = n // heads
    nodes = n * part_rows
    me = lax.axis_index("head")
    side = lax.axis_index("tensor")
    width = go_ref.shape[1]
    loads = [
        pltpu.make_async_copy(src, dst, load_sem.at[at])
        for at, (src, dst) in enumerate(
            ((k_hbm, k_ref), (v_hbm, v_ref), (go_hbm, go_ref), (q_hbm, q_ref), (w_hbm, w_ref))
        )
    ]
    for load in loads:
        load.start()
    barrier = pltpu.get_barrier_semaphore()
    pl.semaphore_signal(barrier, inc=1, device_id={"tensor": 1 - side}, device_id_type=MESH)

    @pl.loop(1, n)
    def _(k):
        pl.semaphore_signal(barrier, inc=1, device_id={"head": lax.rem(me + k, n)}, device_id_type=MESH)

    loads[0].wait()
    loads[1].wait()

    @pl.loop(0, graphs)
    def _(g):
        rows = pl.ds(pl.multiple_of(g * part_rows, part_rows), part_rows)
        for h in range(heads):
            cols = slice(h * HD, (h + 1) * HD)
            kv_pack[g * heads + h, :, :HD] = k_ref[rows, cols]
            kv_pack[g * heads + h, :, HD:] = v_ref[rows, cols]

    loads[2].wait()
    pl.semaphore_wait(barrier, n)
    pair = pltpu.make_async_remote_copy(
        src_ref=go_ref, dst_ref=grad_s, send_sem=pair_sem.at[0], recv_sem=pair_sem.at[1],
        device_id={"tensor": 1 - side}, device_id_type=MESH,
    )
    pair.start()

    def copy_to(which, pack, land, peer, slot):
        return pltpu.make_async_remote_copy(
            src_ref=pack.at[peer], dst_ref=land.at[slot],
            send_sem=send_sem.at[which, peer], recv_sem=recv_sem.at[which, slot],
            device_id={"head": peer}, device_id_type=MESH,
        )

    def send_all(which, pack, land):
        @pl.loop(0, n - 1)
        def _(i):
            copy_to(which, pack, land, lax.rem(me + hop(i, n), n), me).start()

    send_all(0, kv_pack, kv_in)
    loads[3].wait()
    loads[4].wait()
    near = pl.ds(pl.multiple_of(side * width, width), width)
    far = pl.ds(pl.multiple_of((1 - side) * width, width), width)
    attn_s[...] = lax.dot_general(go_ref[...], w_ref[:, near], NT, preferred_element_type=jnp.float32)
    pair.wait()
    attn_s[...] += lax.dot_general(grad_s[...], w_ref[:, far], NT, preferred_element_type=jnp.float32)

    @pl.loop(0, graphs)
    def _(g):
        rows = pl.ds(pl.multiple_of(g * part_rows, part_rows), part_rows)
        for h in range(heads):
            cols = slice(h * HD, (h + 1) * HD)
            qg_pack[g * heads + h, :, :HD] = q_ref[rows, cols]
            qg_pack[g * heads + h, :, HD:] = attn_s[rows, cols].astype(jnp.bfloat16)

    send_all(1, qg_pack, qg_in)

    def gather(which, pack, land, out):
        span = BS * min(WIDE, nodes // BS)
        land[me] = pack[me]
        acc_s[...] = jnp.zeros_like(acc_s)

        @pl.loop(0, n)
        def _(k):
            i = lax.rem(k + n - 1, n)
            source = lax.rem(me + n - hop(i, n), n)

            @pl.when(k > 0)
            def _():
                copy_to(which, pack, land, source, source).wait_recv()

            row = row_ref[source]
            block = marks(row // BS, (PACKED, part_rows))
            ids = lax.broadcasted_iota(jnp.int32, (BS, part_rows), 0)
            same = jnp.where(ids == row % BS, 1.0, 0.0).astype(jnp.bfloat16)
            chunk = land[source]

            @pl.loop(0, nodes // span)
            def _(t):
                hot = []
                for c in range(span // BS):
                    here = block == marks(jnp.full((1, 1), t * (span // BS) + c), (PACKED, part_rows))
                    hot += [jnp.where(here, same[r:r + PACKED], jnp.zeros_like(block)) for r in range(0, BS, PACKED)]
                rows = pl.ds(pl.multiple_of(t * span, span), span)
                acc_s[rows] += dot(jnp.concatenate(hot, axis=0), chunk)

        out[...] = acc_s[...].astype(jnp.bfloat16)

    gather(0, kv_pack, kv_in, kv_out)
    gather(1, qg_pack, qg_in, qg_out)

    @pl.loop(1, n)
    def _(k):
        peer = lax.rem(me + k, n)
        copy_to(0, kv_pack, kv_in, peer, me).wait_send()
        copy_to(1, qg_pack, qg_in, peer, me).wait_send()


def spreading(order, query, keys_in, values_in, grad_out, w_out, n):
    nodes = order.shape[0]
    part_rows = nodes // n
    vmem = pl.BlockSpec(memory_space=pltpu.VMEM)
    chunks = pltpu.VMEM((n, part_rows, 2 * HD), jnp.bfloat16)
    half = jax.ShapeDtypeStruct((nodes, 2 * HD), jnp.bfloat16)
    return pl.pallas_call(
        spread,
        out_shape=(half, half),
        in_specs=[vmem] + [pl.BlockSpec(memory_space=pltpu.HBM)] * 5,
        out_specs=(vmem, vmem),
        scratch_shapes=[
            pltpu.VMEM(query.shape, jnp.bfloat16),
            pltpu.VMEM(query.shape, jnp.bfloat16),
            pltpu.VMEM(query.shape, jnp.bfloat16),
            pltpu.VMEM(grad_out.shape, jnp.bfloat16),
            pltpu.VMEM(w_out.shape, jnp.bfloat16),
            pltpu.SemaphoreType.DMA((5,)),
            pltpu.VMEM(grad_out.shape, jnp.bfloat16),
            pltpu.VMEM(query.shape, jnp.float32),
            chunks, chunks, chunks, chunks,
            pltpu.VMEM((nodes, 2 * HD), jnp.float32),
            pltpu.SemaphoreType.DMA((2,)),
            pltpu.SemaphoreType.DMA((2, n)),
            pltpu.SemaphoreType.DMA((2, n)),
        ],
        compiler_params=pltpu.CompilerParams(
            vmem_limit_bytes=VMEM_BYTES, collective_id=0, has_side_effects=True
        ),
        name="spread",
    )(order.reshape(n, 1, part_rows), query, keys_in, values_in, grad_out, w_out)


def attend(block_ref, count_ref, qg_ref, kv_ref, out_ref, kt_s, qg_s, dkv_s, dqt_s, e_s, d_s, top_s, sum_s, dot_s, task):
    block_count = kv_ref.shape[0]
    slots = block_ref.shape[0]
    groups = top_s.shape[0]
    scale = HD ** (-0.5)
    low = lax.broadcasted_iota(jnp.int32, (BS, 2 * HD), 1) < HD

    width = 4

    def ready(i, t):
        for v in range(width):
            b = i * width + v
            count = count_ref[b]
            for g in range(slots // 2):
                on = (2 * g + 1 < count).astype(jnp.int32)
                task[t] = b + (g << 8) + (on << 12) + (block_ref[2 * g, 0, b] << 16) + (block_ref[2 * g + 1, 0, b] << 24)
                t = t + (2 * g < count).astype(jnp.int32)
            qg = qg_ref[b].astype(jnp.float32)
            qg_s[b, :BS] = jnp.where(low, qg * scale, 0.0).astype(jnp.bfloat16)
            qg_s[b, BS:] = jnp.where(low, 0.0, qg).astype(jnp.bfloat16)
            kt_s[b] = (kv_ref[b].astype(jnp.float32).T[:HD] * scale).astype(jnp.bfloat16)
            dkv_s[b] = jnp.zeros((BS, 2 * HD), jnp.float32)
            dqt_s[b] = jnp.zeros((HD, BS), jnp.float32)
        return t

    total = lax.fori_loop(0, block_count // width, ready, 0)
    for u in range(UNROLL - 1):
        task[total + u] = block_count + (1 << 12)
    trips = (total + UNROLL - 1) // UNROLL

    def read(t):
        code = task[t]
        return code & 255, (code >> 8) & 15, (code >> 12) & 1, [(code >> 16) & 255, (code >> 24) & 255]

    qg_s[block_count] = jnp.zeros((2 * BS, 2 * HD), jnp.bfloat16)
    top_s[...] = jnp.full(top_s.shape, -1e30, jnp.float32)
    sum_s[...] = jnp.zeros(sum_s.shape, jnp.float32)
    dot_s[...] = jnp.zeros(dot_s.shape, jnp.float32)

    def forward(t):
        b, g, on, c = read(t)
        qg = qg_s[b]
        sd = [lax.dot_general(kv_ref[c[k]], qg, NT, preferred_element_type=jnp.float32) for k in (0, 1)]
        s = [sd[0][:, :BS], jnp.where(on > 0, sd[1][:, :BS], -jnp.inf)]
        top = jnp.max(jnp.maximum(s[0], s[1]), axis=0, keepdims=True)
        e = [jnp.exp(x - top) for x in s]
        d = [x[:, BS:] for x in sd]
        for k in (0, 1):
            e_s[2 * t + k] = e[k]
            d_s[2 * t + k] = d[k]
        row = pl.ds(b, 1)
        top_s[g, row] = top
        sum_s[g, row] = jnp.sum(e[0] + e[1], axis=0, keepdims=True)
        dot_s[g, row] = jnp.sum(e[0] * d[0] + e[1] * d[1], axis=0, keepdims=True)

    @pl.loop(0, trips)
    def _(i):
        for u in range(UNROLL):
            forward(i * UNROLL + u)

    tops = [top_s[g] for g in range(groups)]
    top = tops[0]
    for x in tops[1:]:
        top = jnp.maximum(top, x)
    part = [jnp.exp(x - top) for x in tops]
    norm = sum(part[g] * sum_s[g] for g in range(groups))
    inv = 1.0 / norm
    delta = sum(part[g] * dot_s[g] for g in range(groups)) * inv
    for g in range(groups):
        top_s[g] = part[g] * inv
    sum_s[0] = delta

    def backward(t):
        b, g, _, c = read(t)
        qg = qg_s[b]
        row = pl.ds(b, 1)
        factor = top_s[g, row]
        delta = sum_s[0, row]
        ds, upd = [], []
        for k in (0, 1):
            p = e_s[2 * t + k] * factor
            ds.append((p * (d_s[2 * t + k] - delta)).astype(jnp.bfloat16))
            upd.append(dot(jnp.concatenate((ds[k], p.astype(jnp.bfloat16)), axis=1), qg))
        kt = jnp.concatenate((kt_s[c[0]], kt_s[c[1]]), axis=1)
        return b, c, upd, dot(kt, jnp.concatenate(ds, axis=0))

    @pl.loop(0, trips)
    def _(i):
        done = [backward(i * UNROLL + u) for u in range(UNROLL)]
        for b, c, upd, dqt in done:
            for k in (0, 1):
                dkv_s[c[k]] += upd[k]
            dqt_s[b] += dqt

    @pl.loop(0, block_count, unroll=4)
    def _(b):
        rows = pl.ds(pl.multiple_of(b * BS, BS), BS)
        dqt = dqt_s[b]
        out_ref[rows, :2 * HD] = dkv_s[b].astype(jnp.bfloat16)
        out_ref[rows, 2 * HD:] = jnp.concatenate((dqt, dqt), axis=0).T.astype(jnp.bfloat16)

def attention(qg, kv, block_col, count_row):
    nodes = qg.shape[0]
    block_count = nodes // BS
    slots = block_col.shape[0]
    groups = (slots + 1) // 2
    tasks = block_count * groups + UNROLL
    rows = block_count + 8
    vmem = pl.BlockSpec(memory_space=pltpu.VMEM)
    smem = pl.BlockSpec(memory_space=pltpu.SMEM)
    return pl.pallas_call(
        attend,
        out_shape=jax.ShapeDtypeStruct((nodes, 4 * HD), jnp.bfloat16),
        in_specs=[smem, smem, vmem, vmem],
        out_specs=vmem,
        scratch_shapes=[
            pltpu.VMEM((block_count, HD, BS), jnp.bfloat16),
            pltpu.VMEM((block_count + 1, 2 * BS, 2 * HD), jnp.bfloat16),
            pltpu.VMEM((block_count, BS, 2 * HD), jnp.float32),
            pltpu.VMEM((block_count + 1, HD, BS), jnp.float32),
            pltpu.VMEM((2 * tasks, BS, BS), jnp.float32),
            pltpu.VMEM((2 * tasks, BS, BS), jnp.float32),
            pltpu.VMEM((groups, rows, BS), jnp.float32),
            pltpu.VMEM((groups, rows, BS), jnp.float32),
            pltpu.VMEM((groups, rows, BS), jnp.float32),
            pltpu.SMEM((tasks,), jnp.int32),
        ],
        compiler_params=pltpu.CompilerParams(vmem_limit_bytes=VMEM_BYTES),
        name="attend",
    )(block_col, count_row, qg.reshape(block_count, BS, 2 * HD), kv.reshape(block_count, BS, 2 * HD))


def collect(row_ref, g_ref, wq_hbm, wk_hbm, wv_hbm, out_ref,
            wq_ref, wk_ref, wv_ref, load_sem, block_s, spot_s, pack, land, w_s, acc_s, give_s, got_s, pair_sem, send_sem, recv_sem):
    n, out_rows, _ = land.shape
    half = out_rows // 3
    graphs = out_ref.shape[0]
    heads = n // graphs
    nodes = g_ref.shape[0]
    me = lax.axis_index("head")
    side = lax.axis_index("tensor")
    loads = [
        pltpu.make_async_copy(src, dst, load_sem.at[at])
        for at, (src, dst) in enumerate(((wq_hbm, wq_ref), (wk_hbm, wk_ref), (wv_hbm, wv_ref)))
    ]
    for load in loads:
        load.start()
    barrier = pltpu.get_barrier_semaphore()
    pl.semaphore_signal(barrier, inc=1, device_id={"tensor": 1 - side}, device_id_type=MESH)

    @pl.loop(1, n)
    def _(k):
        pl.semaphore_signal(barrier, inc=1, device_id={"head": lax.rem(me + k, n)}, device_id_type=MESH)

    order = row_ref[:, 0, :]
    block_s[...] = (order // BS).astype(jnp.float32).T
    spot_s[...] = (order % BS).astype(jnp.float32).T

    def make(peer, into):
        mine = lax.broadcasted_iota(jnp.int32, (2 * half, n), 1) == peer
        block = marks(jnp.sum(jnp.where(mine, block_s[...], 0.0), axis=1, keepdims=True), (2 * half, BS))
        spot = jnp.sum(jnp.where(mine, spot_s[...], 0.0), axis=1, keepdims=True)
        ids = lax.broadcasted_iota(jnp.int32, (2 * half, BS), 1).astype(jnp.float32)
        same = jnp.where(ids == spot, 1.0, 0.0).astype(jnp.bfloat16)
        hot = [jnp.where(block == jnp.bfloat16(c), same, jnp.zeros_like(same)) for c in range(nodes // BS)]
        got = dot(jnp.concatenate(hot, axis=1), g_ref[...])
        into[:2 * half] = got[:, :2 * HD].astype(jnp.bfloat16)
        low = lax.broadcasted_iota(jnp.int32, (half, 2 * HD), 1) < HD
        into[2 * half:] = jnp.where(low, got[:half, 2 * HD:], got[half:, 2 * HD:]).astype(jnp.bfloat16)

    def copy_to(peer, slot):
        return pltpu.make_async_remote_copy(
            src_ref=pack.at[peer], dst_ref=land.at[slot],
            send_sem=send_sem.at[peer], recv_sem=recv_sem.at[slot],
            device_id={"head": peer}, device_id_type=MESH,
        )

    opposite = lax.rem(me + n // 2, n)
    make(opposite, pack.at[opposite])
    pl.semaphore_wait(barrier, n)
    copy_to(opposite, me).start()

    @pl.loop(1, n - 1)
    def _(i):
        peer = lax.rem(me + hop(i, n), n)
        make(peer, pack.at[peer])
        copy_to(peer, me).start()

    make(me, land.at[me])
    for load in loads:
        load.wait()
    for h in range(heads):
        cols = slice(h * HD, (h + 1) * HD)
        for part in range(2):
            w_s[h, part, :, :HD] = wk_ref[:, cols]
            w_s[h, part, :, HD:2 * HD] = wv_ref[:, cols]
            w_s[h, part, :, (2 + part) * HD:(3 + part) * HD] = wq_ref[:, cols]
            w_s[h, part, :, (3 - part) * HD:(4 - part) * HD] = jnp.zeros((w_s.shape[2], HD), jnp.bfloat16)
    acc_s[...] = jnp.zeros_like(acc_s)

    def project(slot, part):
        rows = pl.ds(pl.multiple_of(part * half, half), half)
        left = jnp.concatenate((land[slot, rows], land[slot, 2 * half:]), axis=1)
        acc_s[slot // heads, part] += lax.dot_general(
            left, w_s[lax.rem(slot, heads), part], NT, preferred_element_type=jnp.float32
        )

    def source_at(k):
        return lax.rem(me + n - hop(lax.rem(k + n - 1, n), n), n)

    @pl.loop(0, n - 1)
    def _(k):
        source = source_at(k)

        @pl.when(k > 0)
        def _():
            copy_to(source, source).wait_recv()

        for part in range(2):
            project(source, part)

    last = source_at(n - 1)
    copy_to(last, last).wait_recv()
    project(last, 1 - side)
    give_s[...] = acc_s[:, 1 - side].astype(jnp.bfloat16)
    pair = pltpu.make_async_remote_copy(
        src_ref=give_s, dst_ref=got_s, send_sem=pair_sem.at[0], recv_sem=pair_sem.at[1],
        device_id={"tensor": 1 - side}, device_id_type=MESH,
    )
    pair.start()
    project(last, side)
    pair.wait()
    out_ref[...] = (acc_s[:, side] + got_s[...].astype(jnp.float32)).astype(jnp.bfloat16)

    @pl.loop(1, n)
    def _(k):
        copy_to(lax.rem(me + k, n), me).wait_send()


def collecting(order, grads, w_query, w_key, w_value, graphs, n):
    nodes = order.shape[0]
    part_rows = nodes // n
    half = part_rows // 2
    full, width = w_query.shape
    heads = width // HD
    vmem = pl.BlockSpec(memory_space=pltpu.VMEM)
    chunks = pltpu.VMEM((n, part_rows * 3 // 2, 2 * HD), jnp.bfloat16)
    result = (graphs, half, full)
    return pl.pallas_call(
        collect,
        out_shape=jax.ShapeDtypeStruct(result, jnp.bfloat16),
        in_specs=[vmem] * 2 + [pl.BlockSpec(memory_space=pltpu.HBM)] * 3,
        out_specs=vmem,
        scratch_shapes=[
            pltpu.VMEM(w_query.shape, jnp.bfloat16),
            pltpu.VMEM(w_query.shape, jnp.bfloat16),
            pltpu.VMEM(w_query.shape, jnp.bfloat16),
            pltpu.SemaphoreType.DMA((3,)),
            pltpu.VMEM((part_rows, n), jnp.float32),
            pltpu.VMEM((part_rows, n), jnp.float32),
            chunks, chunks,
            pltpu.VMEM((heads, 2, full, 4 * HD), jnp.bfloat16),
            pltpu.VMEM((graphs, 2, half, full), jnp.float32),
            pltpu.VMEM(result, jnp.bfloat16),
            pltpu.VMEM(result, jnp.bfloat16),
            pltpu.SemaphoreType.DMA((2,)),
            pltpu.SemaphoreType.DMA((n,)),
            pltpu.SemaphoreType.DMA((n,)),
        ],
        compiler_params=pltpu.CompilerParams(
            vmem_limit_bytes=VMEM_BYTES, collective_id=1, has_side_effects=True
        ),
        name="collect",
    )(order.reshape(n, 1, part_rows), grads, w_query, w_key, w_value)


def on_device(
    query, keys_in, values_in, grad_out, w_out, w_query, w_key, w_value, perm, blocks, counts
):
    local_rows, half_width = query.shape
    graphs, nodes = perm.shape
    half_heads = half_width // HD
    part_rows = local_rows // graphs
    n = nodes // part_rows
    graph = lax.axis_index("head") // half_heads
    order = lax.dynamic_index_in_dim(perm, graph, 0, keepdims=False)
    block_row = lax.dynamic_index_in_dim(blocks.transpose(2, 0, 1), graph, 1)
    count_row = lax.dynamic_index_in_dim(counts, graph, 0, keepdims=False)
    by_graph = [
        member.reshape(part_rows, graphs, half_width).transpose(1, 0, 2).reshape(local_rows, half_width)
        for member in (query, keys_in, values_in, grad_out)
    ]
    qg, kv = spreading(order, *by_graph, w_out, n)
    grads = attention(qg, kv, block_row, count_row)
    total = collecting(order, grads, w_query, w_key, w_value, graphs, n)
    return total.transpose(1, 0, 2).reshape(local_rows // 2, -1)


def solution(mesh):
    return jax.shard_map(
        on_device,
        mesh=mesh,
        in_specs=(
            P(("groups", "head"), "tensor"),
            P(("groups", "head"), "tensor"),
            P(("groups", "head"), "tensor"),
            P(("groups", "head"), "tensor"),
            P("tensor", None),
            P(None, "tensor"),
            P(None, "tensor"),
            P(None, "tensor"),
            P("groups", None),
            P("groups", None, None),
            P("groups", None),
        ),
        out_specs=P(("groups", "head", "tensor"), None),
        check_vma=False,
    )
```

```python
import jax
import jax.numpy as jnp
from jax import lax
from jax.experimental import pallas as pl
from jax.experimental.pallas import tpu as pltpu
from jax.sharding import PartitionSpec as P

HD = 64
BS = 128
NT = (((1,), (1,)), ((), ()))
UNROLL = 12
PACKED = 16
WIDE = 16
VMEM_BYTES = 67043328
MESH = pl.DeviceIdType.MESH


def dot(a, b):
    return jnp.dot(a, b, preferred_element_type=jnp.float32)


def marks(values, shape):
    return jnp.broadcast_to(values.astype(jnp.float32), shape).astype(jnp.bfloat16)


def across(i, k, n):
    out = 0
    bit = 1
    while bit < n:
        a, b = lax.rem(i // bit, 2), lax.rem(k // bit, 2)
        out += (a + b - 2 * a * b) * bit
        bit *= 2
    return out


def spread(row_ref, q_hbm, k_hbm, v_hbm, go_hbm, w_hbm, qg_out, kv_out,
           q_ref, k_ref, v_ref, go_ref, w_ref, load_sem, grad_s, attn_s, kv_pack, qg_pack, kv_in, qg_in, acc_s, pair_sem, send_sem, recv_sem):
    n, part_rows, _ = kv_in.shape
    heads = q_ref.shape[1] // HD
    graphs = n // heads
    nodes = n * part_rows
    me = lax.axis_index("head")
    side = lax.axis_index("tensor")
    width = go_ref.shape[1]
    loads = [
        pltpu.make_async_copy(src, dst, load_sem.at[at])
        for at, (src, dst) in enumerate(
            ((k_hbm, k_ref), (v_hbm, v_ref), (go_hbm, go_ref), (q_hbm, q_ref), (w_hbm, w_ref))
        )
    ]
    for load in loads:
        load.start()
    barrier = pltpu.get_barrier_semaphore()
    pl.semaphore_signal(barrier, inc=1, device_id={"tensor": 1 - side}, device_id_type=MESH)

    @pl.loop(1, n)
    def _(k):
        pl.semaphore_signal(barrier, inc=1, device_id={"head": lax.rem(me + k, n)}, device_id_type=MESH)

    loads[0].wait()
    loads[1].wait()

    @pl.loop(0, graphs)
    def _(g):
        rows = pl.ds(pl.multiple_of(g * part_rows, part_rows), part_rows)
        for h in range(heads):
            cols = slice(h * HD, (h + 1) * HD)
            kv_pack[g * heads + h, :, :HD] = k_ref[rows, cols]
            kv_pack[g * heads + h, :, HD:] = v_ref[rows, cols]

    loads[2].wait()
    pl.semaphore_wait(barrier, n)
    pair = pltpu.make_async_remote_copy(
        src_ref=go_ref, dst_ref=grad_s, send_sem=pair_sem.at[0], recv_sem=pair_sem.at[1],
        device_id={"tensor": 1 - side}, device_id_type=MESH,
    )
    pair.start()

    def copy_to(which, pack, land, peer, slot):
        return pltpu.make_async_remote_copy(
            src_ref=pack.at[peer], dst_ref=land.at[slot],
            send_sem=send_sem.at[which, peer], recv_sem=recv_sem.at[which, slot],
            device_id={"head": peer}, device_id_type=MESH,
        )

    far_count = n // 2

    def send(which, pack, land, k):
        copy_to(which, pack, land, across(me, k, n), me).start()

    def send_near(which, pack, land):
        @pl.loop(1, far_count)
        def _(k):
            send(which, pack, land, k)

    @pl.loop(far_count, n)
    def _(k):
        send(0, kv_pack, kv_in, k)

    send_near(0, kv_pack, kv_in)
    loads[3].wait()
    loads[4].wait()
    near = pl.ds(pl.multiple_of(side * width, width), width)
    far = pl.ds(pl.multiple_of((1 - side) * width, width), width)
    attn_s[...] = lax.dot_general(go_ref[...], w_ref[:, near], NT, preferred_element_type=jnp.float32)
    pair.wait()
    attn_s[...] += lax.dot_general(grad_s[...], w_ref[:, far], NT, preferred_element_type=jnp.float32)

    @pl.loop(0, graphs)
    def _(g):
        rows = pl.ds(pl.multiple_of(g * part_rows, part_rows), part_rows)
        for h in range(heads):
            cols = slice(h * HD, (h + 1) * HD)
            qg_pack[g * heads + h, :, :HD] = q_ref[rows, cols]
            qg_pack[g * heads + h, :, HD:] = attn_s[rows, cols].astype(jnp.bfloat16)

    early = far_count // 2

    @pl.loop(far_count, far_count + early)
    def _(k):
        send(1, qg_pack, qg_in, k)

    send_near(1, qg_pack, qg_in)

    def gather(which, pack, land, out):
        span = BS * min(WIDE, nodes // BS)
        land[me] = pack[me]
        acc_s[...] = jnp.zeros_like(acc_s)

        @pl.loop(0, n)
        def _(k):
            source = across(me, k, n)

            @pl.when(k >= far_count)
            def _():
                copy_to(which, pack, land, source, me).wait_send()
                if which == 0:
                    @pl.when(k + early < n)
                    def _():
                        send(1, qg_pack, qg_in, k + early)

            @pl.when(k > 0)
            def _():
                copy_to(which, pack, land, source, source).wait_recv()

            row = row_ref[source]
            block = marks(row // BS, (PACKED, part_rows))
            ids = lax.broadcasted_iota(jnp.int32, (BS, part_rows), 0)
            same = jnp.where(ids == row % BS, 1.0, 0.0).astype(jnp.bfloat16)
            chunk = land[source]

            @pl.loop(0, nodes // span)
            def _(t):
                hot = []
                for c in range(span // BS):
                    here = block == marks(jnp.full((1, 1), t * (span // BS) + c), (PACKED, part_rows))
                    hot += [jnp.where(here, same[r:r + PACKED], jnp.zeros_like(block)) for r in range(0, BS, PACKED)]
                rows = pl.ds(pl.multiple_of(t * span, span), span)
                acc_s[rows] += dot(jnp.concatenate(hot, axis=0), chunk)

        out[...] = acc_s[...].astype(jnp.bfloat16)

    gather(0, kv_pack, kv_in, kv_out)
    gather(1, qg_pack, qg_in, qg_out)

    @pl.loop(1, far_count)
    def _(k):
        peer = across(me, k, n)
        copy_to(0, kv_pack, kv_in, peer, me).wait_send()
        copy_to(1, qg_pack, qg_in, peer, me).wait_send()


def spreading(order, query, keys_in, values_in, grad_out, w_out, n):
    nodes = order.shape[0]
    part_rows = nodes // n
    vmem = pl.BlockSpec(memory_space=pltpu.VMEM)
    chunks = pltpu.VMEM((n, part_rows, 2 * HD), jnp.bfloat16)
    half = jax.ShapeDtypeStruct((nodes, 2 * HD), jnp.bfloat16)
    return pl.pallas_call(
        spread,
        out_shape=(half, half),
        in_specs=[vmem] + [pl.BlockSpec(memory_space=pltpu.HBM)] * 5,
        out_specs=(vmem, vmem),
        scratch_shapes=[
            pltpu.VMEM(query.shape, jnp.bfloat16),
            pltpu.VMEM(query.shape, jnp.bfloat16),
            pltpu.VMEM(query.shape, jnp.bfloat16),
            pltpu.VMEM(grad_out.shape, jnp.bfloat16),
            pltpu.VMEM(w_out.shape, jnp.bfloat16),
            pltpu.SemaphoreType.DMA((5,)),
            pltpu.VMEM(grad_out.shape, jnp.bfloat16),
            pltpu.VMEM(query.shape, jnp.float32),
            chunks, chunks, chunks, chunks,
            pltpu.VMEM((nodes, 2 * HD), jnp.float32),
            pltpu.SemaphoreType.DMA((2,)),
            pltpu.SemaphoreType.DMA((2, n)),
            pltpu.SemaphoreType.DMA((2, n)),
        ],
        compiler_params=pltpu.CompilerParams(
            vmem_limit_bytes=VMEM_BYTES, collective_id=0, has_side_effects=True
        ),
        name="spread",
    )(order.reshape(n, 1, part_rows), query, keys_in, values_in, grad_out, w_out)


def attend(block_ref, count_ref, qg_ref, kv_ref, out_ref, kt_s, qg_s, dkv_s, dqt_s, e_s, d_s, top_s, sum_s, dot_s, task):
    block_count = kv_ref.shape[0]
    slots = block_ref.shape[0]
    groups = top_s.shape[0]
    scale = HD ** (-0.5)
    low = lax.broadcasted_iota(jnp.int32, (BS, 2 * HD), 1) < HD

    width = 4

    def ready(i, t):
        for v in range(width):
            b = i * width + v
            count = count_ref[b]
            for g in range(slots // 2):
                on = (2 * g + 1 < count).astype(jnp.int32)
                task[t] = b + (g << 8) + (on << 12) + (block_ref[2 * g, 0, b] << 16) + (block_ref[2 * g + 1, 0, b] << 24)
                t = t + (2 * g < count).astype(jnp.int32)
            qg = qg_ref[b].astype(jnp.float32)
            qg_s[b, :BS] = jnp.where(low, qg * scale, 0.0).astype(jnp.bfloat16)
            qg_s[b, BS:] = jnp.where(low, 0.0, qg).astype(jnp.bfloat16)
            kt_s[b] = (kv_ref[b].astype(jnp.float32).T[:HD] * scale).astype(jnp.bfloat16)
            dkv_s[b] = jnp.zeros((BS, 2 * HD), jnp.float32)
            dqt_s[b] = jnp.zeros((HD, BS), jnp.float32)
        return t

    total = lax.fori_loop(0, block_count // width, ready, 0)
    for u in range(UNROLL - 1):
        task[total + u] = block_count + (1 << 12)
    trips = (total + UNROLL - 1) // UNROLL

    def read(t):
        code = task[t]
        return code & 255, (code >> 8) & 15, (code >> 12) & 1, [(code >> 16) & 255, (code >> 24) & 255]

    qg_s[block_count] = jnp.zeros((2 * BS, 2 * HD), jnp.bfloat16)
    top_s[...] = jnp.full(top_s.shape, -1e30, jnp.float32)
    sum_s[...] = jnp.zeros(sum_s.shape, jnp.float32)
    dot_s[...] = jnp.zeros(dot_s.shape, jnp.float32)

    def forward(t):
        b, g, on, c = read(t)
        qg = qg_s[b]
        sd = [lax.dot_general(kv_ref[c[k]], qg, NT, preferred_element_type=jnp.float32) for k in (0, 1)]
        s = [sd[0][:, :BS], jnp.where(on > 0, sd[1][:, :BS], -jnp.inf)]
        top = jnp.max(jnp.maximum(s[0], s[1]), axis=0, keepdims=True)
        e = [jnp.exp(x - top) for x in s]
        d = [x[:, BS:] for x in sd]
        for k in (0, 1):
            e_s[2 * t + k] = e[k]
            d_s[2 * t + k] = d[k]
        row = pl.ds(b, 1)
        top_s[g, row] = top
        sum_s[g, row] = jnp.sum(e[0] + e[1], axis=0, keepdims=True)
        dot_s[g, row] = jnp.sum(e[0] * d[0] + e[1] * d[1], axis=0, keepdims=True)

    @pl.loop(0, trips)
    def _(i):
        for u in range(UNROLL):
            forward(i * UNROLL + u)

    tops = [top_s[g] for g in range(groups)]
    top = tops[0]
    for x in tops[1:]:
        top = jnp.maximum(top, x)
    part = [jnp.exp(x - top) for x in tops]
    norm = sum(part[g] * sum_s[g] for g in range(groups))
    inv = 1.0 / norm
    delta = sum(part[g] * dot_s[g] for g in range(groups)) * inv
    for g in range(groups):
        top_s[g] = part[g] * inv
    sum_s[0] = delta

    def backward(t):
        b, g, _, c = read(t)
        qg = qg_s[b]
        row = pl.ds(b, 1)
        factor = top_s[g, row]
        delta = sum_s[0, row]
        ds, upd = [], []
        for k in (0, 1):
            p = e_s[2 * t + k] * factor
            ds.append((p * (d_s[2 * t + k] - delta)).astype(jnp.bfloat16))
            upd.append(dot(jnp.concatenate((ds[k], p.astype(jnp.bfloat16)), axis=1), qg))
        kt = jnp.concatenate((kt_s[c[0]], kt_s[c[1]]), axis=1)
        return b, c, upd, dot(kt, jnp.concatenate(ds, axis=0))

    @pl.loop(0, trips)
    def _(i):
        done = [backward(i * UNROLL + u) for u in range(UNROLL)]
        for b, c, upd, dqt in done:
            for k in (0, 1):
                dkv_s[c[k]] += upd[k]
            dqt_s[b] += dqt

    @pl.loop(0, block_count, unroll=4)
    def _(b):
        rows = pl.ds(pl.multiple_of(b * BS, BS), BS)
        dqt = dqt_s[b]
        out_ref[rows, :2 * HD] = dkv_s[b].astype(jnp.bfloat16)
        out_ref[rows, 2 * HD:] = jnp.concatenate((dqt, dqt), axis=0).T.astype(jnp.bfloat16)

def attention(qg, kv, block_col, count_row):
    nodes = qg.shape[0]
    block_count = nodes // BS
    slots = block_col.shape[0]
    groups = (slots + 1) // 2
    tasks = block_count * groups + UNROLL
    rows = block_count + 8
    vmem = pl.BlockSpec(memory_space=pltpu.VMEM)
    smem = pl.BlockSpec(memory_space=pltpu.SMEM)
    return pl.pallas_call(
        attend,
        out_shape=jax.ShapeDtypeStruct((nodes, 4 * HD), jnp.bfloat16),
        in_specs=[smem, smem, vmem, vmem],
        out_specs=vmem,
        scratch_shapes=[
            pltpu.VMEM((block_count, HD, BS), jnp.bfloat16),
            pltpu.VMEM((block_count + 1, 2 * BS, 2 * HD), jnp.bfloat16),
            pltpu.VMEM((block_count, BS, 2 * HD), jnp.float32),
            pltpu.VMEM((block_count + 1, HD, BS), jnp.float32),
            pltpu.VMEM((2 * tasks, BS, BS), jnp.float32),
            pltpu.VMEM((2 * tasks, BS, BS), jnp.float32),
            pltpu.VMEM((groups, rows, BS), jnp.float32),
            pltpu.VMEM((groups, rows, BS), jnp.float32),
            pltpu.VMEM((groups, rows, BS), jnp.float32),
            pltpu.SMEM((tasks,), jnp.int32),
        ],
        compiler_params=pltpu.CompilerParams(vmem_limit_bytes=VMEM_BYTES),
        name="attend",
    )(block_col, count_row, qg.reshape(block_count, BS, 2 * HD), kv.reshape(block_count, BS, 2 * HD))


def collect(row_ref, g_ref, wq_hbm, wk_hbm, wv_hbm, out_ref,
            wq_ref, wk_ref, wv_ref, load_sem, block_s, spot_s, pack, land, w_s, acc_s, give_s, got_s, pair_sem, send_sem, recv_sem):
    n, out_rows, _ = land.shape
    half = out_rows // 3
    graphs = out_ref.shape[0]
    heads = n // graphs
    nodes = g_ref.shape[0]
    me = lax.axis_index("head")
    side = lax.axis_index("tensor")
    loads = [
        pltpu.make_async_copy(src, dst, load_sem.at[at])
        for at, (src, dst) in enumerate(((wq_hbm, wq_ref), (wk_hbm, wk_ref), (wv_hbm, wv_ref)))
    ]
    for load in loads:
        load.start()
    barrier = pltpu.get_barrier_semaphore()
    pl.semaphore_signal(barrier, inc=1, device_id={"tensor": 1 - side}, device_id_type=MESH)

    @pl.loop(1, n)
    def _(k):
        pl.semaphore_signal(barrier, inc=1, device_id={"head": lax.rem(me + k, n)}, device_id_type=MESH)

    order = row_ref[:, 0, :]
    block_s[...] = (order // BS).astype(jnp.float32).T
    spot_s[...] = (order % BS).astype(jnp.float32).T

    def make(peer, into):
        mine = lax.broadcasted_iota(jnp.int32, (2 * half, n), 1) == peer
        block = marks(jnp.sum(jnp.where(mine, block_s[...], 0.0), axis=1, keepdims=True), (2 * half, BS))
        spot = jnp.sum(jnp.where(mine, spot_s[...], 0.0), axis=1, keepdims=True)
        ids = lax.broadcasted_iota(jnp.int32, (2 * half, BS), 1).astype(jnp.float32)
        same = jnp.where(ids == spot, 1.0, 0.0).astype(jnp.bfloat16)
        hot = [jnp.where(block == jnp.bfloat16(c), same, jnp.zeros_like(same)) for c in range(nodes // BS)]
        got = dot(jnp.concatenate(hot, axis=1), g_ref[...])
        into[:2 * half] = got[:, :2 * HD].astype(jnp.bfloat16)
        low = lax.broadcasted_iota(jnp.int32, (half, 2 * HD), 1) < HD
        into[2 * half:] = jnp.where(low, got[:half, 2 * HD:], got[half:, 2 * HD:]).astype(jnp.bfloat16)

    def copy_to(peer, slot):
        return pltpu.make_async_remote_copy(
            src_ref=pack.at[peer], dst_ref=land.at[slot],
            send_sem=send_sem.at[peer], recv_sem=recv_sem.at[slot],
            device_id={"head": peer}, device_id_type=MESH,
        )

    far_count = n // 2

    def serve(peer):
        make(peer, pack.at[peer])
        copy_to(peer, me).start()

    first = across(me, far_count, n)
    make(first, pack.at[first])
    pl.semaphore_wait(barrier, n)
    copy_to(first, me).start()

    @pl.loop(far_count + 1, n)
    def _(k):
        serve(across(me, k, n))

    @pl.loop(1, far_count)
    def _(k):
        serve(across(me, k, n))

    make(me, land.at[me])
    for load in loads:
        load.wait()
    for h in range(heads):
        cols = slice(h * HD, (h + 1) * HD)
        for part in range(2):
            w_s[h, part, :, :HD] = wk_ref[:, cols]
            w_s[h, part, :, HD:2 * HD] = wv_ref[:, cols]
            w_s[h, part, :, (2 + part) * HD:(3 + part) * HD] = wq_ref[:, cols]
            w_s[h, part, :, (3 - part) * HD:(4 - part) * HD] = jnp.zeros((w_s.shape[2], HD), jnp.bfloat16)
    acc_s[...] = jnp.zeros_like(acc_s)

    def project(slot, part):
        rows = pl.ds(pl.multiple_of(part * half, half), half)
        left = jnp.concatenate((land[slot, rows], land[slot, 2 * half:]), axis=1)
        acc_s[slot // heads, part] += lax.dot_general(
            left, w_s[lax.rem(slot, heads), part], NT, preferred_element_type=jnp.float32
        )

    @pl.loop(0, n - 1)
    def _(k):
        source = across(me, k, n)

        @pl.when(k > 0)
        def _():
            copy_to(source, source).wait_recv()

        for part in range(2):
            project(source, part)

    last = across(me, n - 1, n)
    copy_to(last, last).wait_recv()
    project(last, 1 - side)
    give_s[...] = acc_s[:, 1 - side].astype(jnp.bfloat16)
    pair = pltpu.make_async_remote_copy(
        src_ref=give_s, dst_ref=got_s, send_sem=pair_sem.at[0], recv_sem=pair_sem.at[1],
        device_id={"tensor": 1 - side}, device_id_type=MESH,
    )
    pair.start()
    project(last, side)
    pair.wait()
    out_ref[...] = (acc_s[:, side] + got_s[...].astype(jnp.float32)).astype(jnp.bfloat16)

    @pl.loop(1, n)
    def _(k):
        copy_to(lax.rem(me + k, n), me).wait_send()


def collecting(order, grads, w_query, w_key, w_value, graphs, n):
    nodes = order.shape[0]
    part_rows = nodes // n
    half = part_rows // 2
    full, width = w_query.shape
    heads = width // HD
    vmem = pl.BlockSpec(memory_space=pltpu.VMEM)
    chunks = pltpu.VMEM((n, part_rows * 3 // 2, 2 * HD), jnp.bfloat16)
    result = (graphs, half, full)
    return pl.pallas_call(
        collect,
        out_shape=jax.ShapeDtypeStruct(result, jnp.bfloat16),
        in_specs=[vmem] * 2 + [pl.BlockSpec(memory_space=pltpu.HBM)] * 3,
        out_specs=vmem,
        scratch_shapes=[
            pltpu.VMEM(w_query.shape, jnp.bfloat16),
            pltpu.VMEM(w_query.shape, jnp.bfloat16),
            pltpu.VMEM(w_query.shape, jnp.bfloat16),
            pltpu.SemaphoreType.DMA((3,)),
            pltpu.VMEM((part_rows, n), jnp.float32),
            pltpu.VMEM((part_rows, n), jnp.float32),
            chunks, chunks,
            pltpu.VMEM((heads, 2, full, 4 * HD), jnp.bfloat16),
            pltpu.VMEM((graphs, 2, half, full), jnp.float32),
            pltpu.VMEM(result, jnp.bfloat16),
            pltpu.VMEM(result, jnp.bfloat16),
            pltpu.SemaphoreType.DMA((2,)),
            pltpu.SemaphoreType.DMA((n,)),
            pltpu.SemaphoreType.DMA((n,)),
        ],
        compiler_params=pltpu.CompilerParams(
            vmem_limit_bytes=VMEM_BYTES, collective_id=1, has_side_effects=True
        ),
        name="collect",
    )(order.reshape(n, 1, part_rows), grads, w_query, w_key, w_value)


def on_device(
    query, keys_in, values_in, grad_out, w_out, w_query, w_key, w_value, perm, blocks, counts
):
    local_rows, half_width = query.shape
    graphs, nodes = perm.shape
    half_heads = half_width // HD
    part_rows = local_rows // graphs
    n = nodes // part_rows
    graph = lax.axis_index("head") // half_heads
    order = lax.dynamic_index_in_dim(perm, graph, 0, keepdims=False)
    block_row = lax.dynamic_index_in_dim(blocks.transpose(2, 0, 1), graph, 1)
    count_row = lax.dynamic_index_in_dim(counts, graph, 0, keepdims=False)
    by_graph = [
        member.reshape(part_rows, graphs, half_width).transpose(1, 0, 2).reshape(local_rows, half_width)
        for member in (query, keys_in, values_in, grad_out)
    ]
    qg, kv = spreading(order, *by_graph, w_out, n)
    grads = attention(qg, kv, block_row, count_row)
    total = collecting(order, grads, w_query, w_key, w_value, graphs, n)
    return total.transpose(1, 0, 2).reshape(local_rows // 2, -1)


def solution(mesh):
    return jax.shard_map(
        on_device,
        mesh=mesh,
        in_specs=(
            P(("groups", "head"), "tensor"),
            P(("groups", "head"), "tensor"),
            P(("groups", "head"), "tensor"),
            P(("groups", "head"), "tensor"),
            P("tensor", None),
            P(None, "tensor"),
            P(None, "tensor"),
            P(None, "tensor"),
            P("groups", None),
            P("groups", None, None),
            P("groups", None),
        ),
        out_specs=P(("groups", "head", "tensor"), None),
        check_vma=False,
    )
```

```python
import jax
import jax.numpy as jnp
from jax import lax
from jax.experimental import pallas as pl
from jax.experimental.pallas import tpu as pltpu
from jax.sharding import PartitionSpec as P

HD = 64
BS = 128
NT = (((1,), (1,)), ((), ()))
UNROLL = 12
ROUNDS = 2
PACKED = 16
WIDE = 16
SPREAD_BYTES = 25165824
ATTEND_BYTES = 44040192
COLLECT_BYTES = 33554432
MESH = pl.DeviceIdType.MESH


def dot(a, b):
    return jnp.dot(a, b, preferred_element_type=jnp.float32)


def in_hbm(*arrays):
    return [pltpu.with_memory_space_constraint(x, pltpu.HBM) for x in arrays]


def marks(values, shape):
    return jnp.broadcast_to(values.astype(jnp.float32), shape).astype(jnp.bfloat16)


def across(i, k, n):
    out = 0
    bit = 1
    while bit < n:
        a, b = lax.rem(i // bit, 2), lax.rem(k // bit, 2)
        out += (a + b - 2 * a * b) * bit
        bit *= 2
    return out


def spread(row_hbm, q_hbm, k_hbm, v_hbm, go_hbm, w_hbm, qg_out, kv_out,
           row_ref, q_ref, k_ref, v_ref, go_ref, w_ref, load_sem, grad_s, attn_s, kv_pack, qg_pack, kv_in, qg_in, acc_s, pair_sem, send_sem, recv_sem):
    n, part_rows, _ = kv_in.shape
    heads = q_ref.shape[1] // HD
    graphs = n // heads
    nodes = n * part_rows
    me = lax.axis_index("head")
    side = lax.axis_index("tensor")
    width = go_ref.shape[1]
    loads = [
        pltpu.make_async_copy(src, dst, load_sem.at[at])
        for at, (src, dst) in enumerate(
            ((k_hbm, k_ref), (v_hbm, v_ref), (go_hbm, go_ref), (q_hbm, q_ref), (w_hbm, w_ref), (row_hbm, row_ref))
        )
    ]
    for load in loads:
        load.start()
    barrier = pltpu.get_barrier_semaphore()
    pl.semaphore_signal(barrier, inc=1, device_id={"tensor": 1 - side}, device_id_type=MESH)

    @pl.loop(1, n)
    def _(k):
        pl.semaphore_signal(barrier, inc=1, device_id={"head": lax.rem(me + k, n)}, device_id_type=MESH)

    loads[0].wait()
    loads[1].wait()

    @pl.loop(0, graphs)
    def _(g):
        rows = pl.ds(pl.multiple_of(g * part_rows, part_rows), part_rows)
        for h in range(heads):
            cols = slice(h * HD, (h + 1) * HD)
            kv_pack[g * heads + h, :, :HD] = k_ref[rows, cols]
            kv_pack[g * heads + h, :, HD:] = v_ref[rows, cols]

    loads[2].wait()
    pl.semaphore_wait(barrier, n)
    pair = pltpu.make_async_remote_copy(
        src_ref=go_ref, dst_ref=grad_s, send_sem=pair_sem.at[0], recv_sem=pair_sem.at[1],
        device_id={"tensor": 1 - side}, device_id_type=MESH,
    )
    pair.start()

    def copy_to(which, pack, land, peer, slot):
        return pltpu.make_async_remote_copy(
            src_ref=pack.at[peer], dst_ref=land.at[slot],
            send_sem=send_sem.at[which, peer], recv_sem=recv_sem.at[which, slot],
            device_id={"head": peer}, device_id_type=MESH,
        )

    far_count = n // 2

    def send(which, pack, land, k):
        copy_to(which, pack, land, across(me, k, n), me).start()

    def send_near(which, pack, land):
        @pl.loop(1, far_count)
        def _(k):
            send(which, pack, land, k)

    @pl.loop(far_count, n)
    def _(k):
        send(0, kv_pack, kv_in, k)

    send_near(0, kv_pack, kv_in)
    loads[3].wait()
    loads[4].wait()
    loads[5].wait()
    near = pl.ds(pl.multiple_of(side * width, width), width)
    far = pl.ds(pl.multiple_of((1 - side) * width, width), width)
    attn_s[...] = lax.dot_general(go_ref[...], w_ref[:, near], NT, preferred_element_type=jnp.float32)
    pair.wait()
    attn_s[...] += lax.dot_general(grad_s[...], w_ref[:, far], NT, preferred_element_type=jnp.float32)

    @pl.loop(0, graphs)
    def _(g):
        rows = pl.ds(pl.multiple_of(g * part_rows, part_rows), part_rows)
        for h in range(heads):
            cols = slice(h * HD, (h + 1) * HD)
            qg_pack[g * heads + h, :, :HD] = q_ref[rows, cols]
            qg_pack[g * heads + h, :, HD:] = attn_s[rows, cols].astype(jnp.bfloat16)

    early = far_count // 2

    @pl.loop(far_count, far_count + early)
    def _(k):
        send(1, qg_pack, qg_in, k)

    send_near(1, qg_pack, qg_in)

    def gather(which, pack, land, out):
        span = BS * min(WIDE, nodes // BS)
        land[me] = pack[me]
        acc_s[...] = jnp.zeros_like(acc_s)

        @pl.loop(0, n)
        def _(k):
            source = across(me, k, n)

            @pl.when(k >= far_count)
            def _():
                copy_to(which, pack, land, source, me).wait_send()
                if which == 0:
                    @pl.when(k + early < n)
                    def _():
                        send(1, qg_pack, qg_in, k + early)

            @pl.when(k > 0)
            def _():
                copy_to(which, pack, land, source, source).wait_recv()

            row = row_ref[source]
            block = marks(row // BS, (PACKED, part_rows))
            ids = lax.broadcasted_iota(jnp.int32, (BS, part_rows), 0)
            same = jnp.where(ids == row % BS, 1.0, 0.0).astype(jnp.bfloat16)
            chunk = land[source]

            @pl.loop(0, nodes // span)
            def _(t):
                hot = []
                for c in range(span // BS):
                    here = block == marks(jnp.full((1, 1), t * (span // BS) + c), (PACKED, part_rows))
                    hot += [jnp.where(here, same[r:r + PACKED], jnp.zeros_like(block)) for r in range(0, BS, PACKED)]
                rows = pl.ds(pl.multiple_of(t * span, span), span)
                acc_s[rows] += dot(jnp.concatenate(hot, axis=0), chunk)

        out[...] = acc_s[...].astype(jnp.bfloat16)

    gather(0, kv_pack, kv_in, kv_out)
    gather(1, qg_pack, qg_in, qg_out)

    @pl.loop(1, far_count)
    def _(k):
        peer = across(me, k, n)
        copy_to(0, kv_pack, kv_in, peer, me).wait_send()
        copy_to(1, qg_pack, qg_in, peer, me).wait_send()


def spreading(order, query, keys_in, values_in, grad_out, w_out, n):
    nodes = order.shape[0]
    part_rows = nodes // n
    vmem = pl.BlockSpec(memory_space=pltpu.VMEM)
    chunks = pltpu.VMEM((n, part_rows, 2 * HD), jnp.bfloat16)
    half = jax.ShapeDtypeStruct((nodes, 2 * HD), jnp.bfloat16)
    return pl.pallas_call(
        spread,
        out_shape=(half, half),
        in_specs=[pl.BlockSpec(memory_space=pltpu.HBM)] * 6,
        out_specs=(vmem, vmem),
        scratch_shapes=[
            pltpu.VMEM((n, 1, part_rows), jnp.int32),
            pltpu.VMEM(query.shape, jnp.bfloat16),
            pltpu.VMEM(query.shape, jnp.bfloat16),
            pltpu.VMEM(query.shape, jnp.bfloat16),
            pltpu.VMEM(grad_out.shape, jnp.bfloat16),
            pltpu.VMEM(w_out.shape, jnp.bfloat16),
            pltpu.SemaphoreType.DMA((6,)),
            pltpu.VMEM(grad_out.shape, jnp.bfloat16),
            pltpu.VMEM(query.shape, jnp.float32),
            chunks, chunks, chunks, chunks,
            pltpu.VMEM((nodes, 2 * HD), jnp.float32),
            pltpu.SemaphoreType.DMA((2,)),
            pltpu.SemaphoreType.DMA((2, n)),
            pltpu.SemaphoreType.DMA((2, n)),
        ],
        compiler_params=pltpu.CompilerParams(
            vmem_limit_bytes=SPREAD_BYTES, collective_id=0, has_side_effects=True
        ),
        name="spread",
    )(*in_hbm(order.reshape(n, 1, part_rows), query, keys_in, values_in, grad_out, w_out))


def attend(block_ref, count_ref, qg_ref, kv_ref, out_ref, kt_s, qg_s, dkv_s, dqt_s, e_s, d_s, top_s, sum_s, dot_s, task, trips):
    block_count = kv_ref.shape[0]
    slots = block_ref.shape[0]
    groups = top_s.shape[1]
    span = task.shape[0] // ROUNDS
    share = block_count // ROUNDS
    scale = HD ** (-0.5)
    low = lax.broadcasted_iota(jnp.int32, (BS, 2 * HD), 1) < HD

    width = 4

    def ready(i, t):
        for v in range(width):
            b = i * width + v
            count = count_ref[b]
            for g in range(slots // 2):
                on = (2 * g + 1 < count).astype(jnp.int32)
                task[t] = b + (g << 8) + (on << 12) + (block_ref[2 * g, 0, b] << 16) + (block_ref[2 * g + 1, 0, b] << 24)
                t = t + (2 * g < count).astype(jnp.int32)
            qg = qg_ref[b].astype(jnp.float32)
            qg_s[b, :BS] = jnp.where(low, qg * scale, 0.0).astype(jnp.bfloat16)
            qg_s[b, BS:] = jnp.where(low, 0.0, qg).astype(jnp.bfloat16)
            kt_s[b] = (kv_ref[b].astype(jnp.float32).T[:HD] * scale).astype(jnp.bfloat16)
            dkv_s[b] = jnp.zeros((BS, 2 * HD), jnp.float32)
            dqt_s[b] = jnp.zeros((HD, BS), jnp.float32)
        return t

    for r in range(ROUNDS):
        total = lax.fori_loop(r * share // width, (r + 1) * share // width, ready, r * span)
        for u in range(UNROLL - 1):
            task[total + u] = block_count + (1 << 12)
        trips[r] = (total - r * span + UNROLL - 1) // UNROLL

    def read(r, t):
        code = task[r * span + t]
        return code & 255, (code >> 8) & 15, (code >> 12) & 1, [(code >> 16) & 255, (code >> 24) & 255]

    qg_s[block_count] = jnp.zeros((2 * BS, 2 * HD), jnp.bfloat16)
    top_s[...] = jnp.full(top_s.shape, -1e30, jnp.float32)
    sum_s[...] = jnp.zeros(sum_s.shape, jnp.float32)
    dot_s[...] = jnp.zeros(dot_s.shape, jnp.float32)

    def forward(r, t):
        b, g, on, c = read(r, t)
        qg = qg_s[b]
        sd = [lax.dot_general(kv_ref[c[k]], qg, NT, preferred_element_type=jnp.float32) for k in (0, 1)]
        s = [sd[0][:, :BS], jnp.where(on > 0, sd[1][:, :BS], -jnp.inf)]
        top = jnp.max(jnp.maximum(s[0], s[1]), axis=0, keepdims=True)
        e = [jnp.exp(x - top) for x in s]
        d = [x[:, BS:] for x in sd]
        for k in (0, 1):
            e_s[2 * t + k] = e[k]
            d_s[2 * t + k] = d[k]
        row = pl.ds(b, 1)
        top_s[r, g, row] = top
        sum_s[r, g, row] = jnp.sum(e[0] + e[1], axis=0, keepdims=True)
        dot_s[r, g, row] = jnp.sum(e[0] * d[0] + e[1] * d[1], axis=0, keepdims=True)

    def backward(r, t):
        b, g, _, c = read(r, t)
        qg = qg_s[b]
        row = pl.ds(b, 1)
        factor = top_s[r, g, row]
        delta = sum_s[r, 0, row]
        ds, upd = [], []
        for k in (0, 1):
            p = e_s[2 * t + k] * factor
            ds.append((p * (d_s[2 * t + k] - delta)).astype(jnp.bfloat16))
            upd.append(dot(jnp.concatenate((ds[k], p.astype(jnp.bfloat16)), axis=1), qg))
        kt = jnp.concatenate((kt_s[c[0]], kt_s[c[1]]), axis=1)
        return b, c, upd, dot(kt, jnp.concatenate(ds, axis=0))

    @pl.loop(0, ROUNDS)
    def _(r):
        @pl.loop(0, trips[r])
        def _(i):
            for u in range(UNROLL):
                forward(r, i * UNROLL + u)

        tops = [top_s[r, g] for g in range(groups)]
        top = tops[0]
        for x in tops[1:]:
            top = jnp.maximum(top, x)
        part = [jnp.exp(x - top) for x in tops]
        inv = 1.0 / sum(part[g] * sum_s[r, g] for g in range(groups))
        delta = sum(part[g] * dot_s[r, g] for g in range(groups)) * inv
        for g in range(groups):
            top_s[r, g] = part[g] * inv
        sum_s[r, 0] = delta

        @pl.loop(0, trips[r])
        def _(i):
            done = [backward(r, i * UNROLL + u) for u in range(UNROLL)]
            for b, c, upd, dqt in done:
                for k in (0, 1):
                    dkv_s[c[k]] += upd[k]
                dqt_s[b] += dqt

    @pl.loop(0, block_count, unroll=4)
    def _(b):
        rows = pl.ds(pl.multiple_of(b * BS, BS), BS)
        dqt = dqt_s[b]
        out_ref[rows, :2 * HD] = dkv_s[b].astype(jnp.bfloat16)
        out_ref[rows, 2 * HD:] = jnp.concatenate((dqt, dqt), axis=0).T.astype(jnp.bfloat16)

def attention(qg, kv, block_col, count_row):
    nodes = qg.shape[0]
    block_count = nodes // BS
    slots = block_col.shape[0]
    groups = (slots + 1) // 2
    tasks = block_count // ROUNDS * groups + UNROLL
    rows = block_count + 8
    vmem = pl.BlockSpec(memory_space=pltpu.VMEM)
    smem = pl.BlockSpec(memory_space=pltpu.SMEM)
    return pl.pallas_call(
        attend,
        out_shape=jax.ShapeDtypeStruct((nodes, 4 * HD), jnp.bfloat16),
        in_specs=[smem, smem, vmem, vmem],
        out_specs=vmem,
        scratch_shapes=[
            pltpu.VMEM((block_count, HD, BS), jnp.bfloat16),
            pltpu.VMEM((block_count + 1, 2 * BS, 2 * HD), jnp.bfloat16),
            pltpu.VMEM((block_count, BS, 2 * HD), jnp.float32),
            pltpu.VMEM((block_count + 1, HD, BS), jnp.float32),
            pltpu.VMEM((2 * tasks, BS, BS), jnp.float32),
            pltpu.VMEM((2 * tasks, BS, BS), jnp.float32),
            pltpu.VMEM((ROUNDS, groups, rows, BS), jnp.float32),
            pltpu.VMEM((ROUNDS, groups, rows, BS), jnp.float32),
            pltpu.VMEM((ROUNDS, groups, rows, BS), jnp.float32),
            pltpu.SMEM((ROUNDS * tasks,), jnp.int32),
            pltpu.SMEM((ROUNDS,), jnp.int32),
        ],
        compiler_params=pltpu.CompilerParams(vmem_limit_bytes=ATTEND_BYTES),
        name="attend",
    )(block_col, count_row, qg.reshape(block_count, BS, 2 * HD), kv.reshape(block_count, BS, 2 * HD))


def collect(row_ref, g_ref, wq_hbm, wk_hbm, wv_hbm, out_ref,
            wq_ref, wk_ref, wv_ref, load_sem, block_s, spot_s, pack, land, w_s, acc_s, give_s, got_s, pair_sem, send_sem, recv_sem):
    n, out_rows, _ = land.shape
    half = out_rows // 3
    graphs = out_ref.shape[0]
    heads = n // graphs
    nodes = g_ref.shape[0]
    me = lax.axis_index("head")
    side = lax.axis_index("tensor")
    loads = [
        pltpu.make_async_copy(src, dst, load_sem.at[at])
        for at, (src, dst) in enumerate(((wq_hbm, wq_ref), (wk_hbm, wk_ref), (wv_hbm, wv_ref)))
    ]
    for load in loads:
        load.start()
    barrier = pltpu.get_barrier_semaphore()
    pl.semaphore_signal(barrier, inc=1, device_id={"tensor": 1 - side}, device_id_type=MESH)

    @pl.loop(1, n)
    def _(k):
        pl.semaphore_signal(barrier, inc=1, device_id={"head": lax.rem(me + k, n)}, device_id_type=MESH)

    order = row_ref[:, 0, :]
    block_s[...] = (order // BS).astype(jnp.float32).T
    spot_s[...] = (order % BS).astype(jnp.float32).T

    def make(peer, into):
        mine = lax.broadcasted_iota(jnp.int32, (2 * half, n), 1) == peer
        block = marks(jnp.sum(jnp.where(mine, block_s[...], 0.0), axis=1, keepdims=True), (2 * half, BS))
        spot = jnp.sum(jnp.where(mine, spot_s[...], 0.0), axis=1, keepdims=True)
        ids = lax.broadcasted_iota(jnp.int32, (2 * half, BS), 1).astype(jnp.float32)
        same = jnp.where(ids == spot, 1.0, 0.0).astype(jnp.bfloat16)
        hot = [jnp.where(block == jnp.bfloat16(c), same, jnp.zeros_like(same)) for c in range(nodes // BS)]
        got = dot(jnp.concatenate(hot, axis=1), g_ref[...])
        into[:2 * half] = got[:, :2 * HD].astype(jnp.bfloat16)
        low = lax.broadcasted_iota(jnp.int32, (half, 2 * HD), 1) < HD
        into[2 * half:] = jnp.where(low, got[:half, 2 * HD:], got[half:, 2 * HD:]).astype(jnp.bfloat16)

    def copy_to(peer, slot):
        return pltpu.make_async_remote_copy(
            src_ref=pack.at[peer], dst_ref=land.at[slot],
            send_sem=send_sem.at[peer], recv_sem=recv_sem.at[slot],
            device_id={"head": peer}, device_id_type=MESH,
        )

    far_count = n // 2

    def serve(peer):
        make(peer, pack.at[peer])
        copy_to(peer, me).start()

    first = across(me, far_count, n)
    make(first, pack.at[first])
    pl.semaphore_wait(barrier, n)
    copy_to(first, me).start()

    @pl.loop(far_count + 1, n)
    def _(k):
        serve(across(me, k, n))

    @pl.loop(1, far_count)
    def _(k):
        serve(across(me, k, n))

    make(me, land.at[me])
    for load in loads:
        load.wait()
    for h in range(heads):
        cols = slice(h * HD, (h + 1) * HD)
        for part in range(2):
            w_s[h, part, :, :HD] = wk_ref[:, cols]
            w_s[h, part, :, HD:2 * HD] = wv_ref[:, cols]
            w_s[h, part, :, (2 + part) * HD:(3 + part) * HD] = wq_ref[:, cols]
            w_s[h, part, :, (3 - part) * HD:(4 - part) * HD] = jnp.zeros((w_s.shape[2], HD), jnp.bfloat16)
    acc_s[...] = jnp.zeros_like(acc_s)

    def project(slot, part):
        rows = pl.ds(pl.multiple_of(part * half, half), half)
        left = jnp.concatenate((land[slot, rows], land[slot, 2 * half:]), axis=1)
        acc_s[slot // heads, part] += lax.dot_general(
            left, w_s[lax.rem(slot, heads), part], NT, preferred_element_type=jnp.float32
        )

    @pl.loop(0, n - 1)
    def _(k):
        source = across(me, k, n)

        @pl.when(k > 0)
        def _():
            copy_to(source, source).wait_recv()

        for part in range(2):
            project(source, part)

    last = across(me, n - 1, n)
    copy_to(last, last).wait_recv()
    project(last, 1 - side)
    give_s[...] = acc_s[:, 1 - side].astype(jnp.bfloat16)
    pair = pltpu.make_async_remote_copy(
        src_ref=give_s, dst_ref=got_s, send_sem=pair_sem.at[0], recv_sem=pair_sem.at[1],
        device_id={"tensor": 1 - side}, device_id_type=MESH,
    )
    pair.start()
    project(last, side)
    pair.wait()
    out_ref[...] = (acc_s[:, side] + got_s[...].astype(jnp.float32)).astype(jnp.bfloat16)

    @pl.loop(1, n)
    def _(k):
        copy_to(lax.rem(me + k, n), me).wait_send()


def collecting(order, grads, w_query, w_key, w_value, graphs, n):
    nodes = order.shape[0]
    part_rows = nodes // n
    half = part_rows // 2
    full, width = w_query.shape
    heads = width // HD
    vmem = pl.BlockSpec(memory_space=pltpu.VMEM)
    chunks = pltpu.VMEM((n, part_rows * 3 // 2, 2 * HD), jnp.bfloat16)
    result = (graphs, half, full)
    return pl.pallas_call(
        collect,
        out_shape=jax.ShapeDtypeStruct(result, jnp.bfloat16),
        in_specs=[vmem] * 2 + [pl.BlockSpec(memory_space=pltpu.HBM)] * 3,
        out_specs=vmem,
        scratch_shapes=[
            pltpu.VMEM(w_query.shape, jnp.bfloat16),
            pltpu.VMEM(w_query.shape, jnp.bfloat16),
            pltpu.VMEM(w_query.shape, jnp.bfloat16),
            pltpu.SemaphoreType.DMA((3,)),
            pltpu.VMEM((part_rows, n), jnp.float32),
            pltpu.VMEM((part_rows, n), jnp.float32),
            chunks, chunks,
            pltpu.VMEM((heads, 2, full, 4 * HD), jnp.bfloat16),
            pltpu.VMEM((graphs, 2, half, full), jnp.float32),
            pltpu.VMEM(result, jnp.bfloat16),
            pltpu.VMEM(result, jnp.bfloat16),
            pltpu.SemaphoreType.DMA((2,)),
            pltpu.SemaphoreType.DMA((n,)),
            pltpu.SemaphoreType.DMA((n,)),
        ],
        compiler_params=pltpu.CompilerParams(
            vmem_limit_bytes=COLLECT_BYTES, collective_id=1, has_side_effects=True
        ),
        name="collect",
    )(order.reshape(n, 1, part_rows), grads, *in_hbm(w_query, w_key, w_value))


def on_device(
    query, keys_in, values_in, grad_out, w_out, w_query, w_key, w_value, perm, blocks, counts
):
    local_rows, half_width = query.shape
    graphs, nodes = perm.shape
    half_heads = half_width // HD
    part_rows = local_rows // graphs
    n = nodes // part_rows
    graph = lax.axis_index("head") // half_heads
    order = lax.dynamic_index_in_dim(perm, graph, 0, keepdims=False)
    block_row = lax.dynamic_index_in_dim(blocks.transpose(2, 0, 1), graph, 1)
    count_row = lax.dynamic_index_in_dim(counts, graph, 0, keepdims=False)
    by_graph = [
        member.reshape(part_rows, graphs, half_width).transpose(1, 0, 2).reshape(local_rows, half_width)
        for member in (query, keys_in, values_in, grad_out)
    ]
    qg, kv = spreading(order, *by_graph, w_out, n)
    grads = attention(qg, kv, block_row, count_row)
    total = collecting(order, grads, w_query, w_key, w_value, graphs, n)
    return total.transpose(1, 0, 2).reshape(local_rows // 2, -1)


def solution(mesh):
    return jax.shard_map(
        on_device,
        mesh=mesh,
        in_specs=(
            P(("groups", "head"), "tensor"),
            P(("groups", "head"), "tensor"),
            P(("groups", "head"), "tensor"),
            P(("groups", "head"), "tensor"),
            P("tensor", None),
            P(None, "tensor"),
            P(None, "tensor"),
            P(None, "tensor"),
            P("groups", None),
            P("groups", None, None),
            P("groups", None),
        ),
        out_specs=P(("groups", "head", "tensor"), None),
        check_vma=False,
    )
```

```python
import jax
import jax.numpy as jnp
from jax import lax
from jax.experimental import pallas as pl
from jax.experimental.pallas import tpu as pltpu
from jax.sharding import PartitionSpec as P

HD = 64
BS = 128
NT = (((1,), (1,)), ((), ()))
UNROLL = 16
ROUNDS = 2
PACKED = 16
WIDE = 16
SPREAD_BYTES = 25165824
ATTEND_BYTES = 44040192
COLLECT_BYTES = 33554432
MESH = pl.DeviceIdType.MESH


def dot(a, b):
    return jnp.dot(a, b, preferred_element_type=jnp.float32)


def in_hbm(*arrays):
    return [pltpu.with_memory_space_constraint(x, pltpu.HBM) for x in arrays]


def marks(values, shape):
    return jnp.broadcast_to(values.astype(jnp.float32), shape).astype(jnp.bfloat16)


def across(i, k, n):
    out = 0
    bit = 1
    while bit < n:
        a, b = lax.rem(i // bit, 2), lax.rem(k // bit, 2)
        out += (a + b - 2 * a * b) * bit
        bit *= 2
    return out


def spread(row_hbm, q_hbm, k_hbm, v_hbm, go_hbm, w_hbm, qg_out, kv_out,
           row_ref, q_ref, k_ref, v_ref, go_ref, w_ref, load_sem, grad_s, attn_s, kv_pack, qg_pack, kv_in, qg_in, acc_s, pair_sem, send_sem, recv_sem):
    n, part_rows, _ = kv_in.shape
    heads = q_ref.shape[1] // HD
    graphs = n // heads
    nodes = n * part_rows
    me = lax.axis_index("head")
    side = lax.axis_index("tensor")
    width = go_ref.shape[1]
    loads = [
        pltpu.make_async_copy(src, dst, load_sem.at[at])
        for at, (src, dst) in enumerate(
            ((k_hbm, k_ref), (v_hbm, v_ref), (go_hbm, go_ref), (q_hbm, q_ref), (w_hbm, w_ref), (row_hbm, row_ref))
        )
    ]
    for load in loads:
        load.start()
    barrier = pltpu.get_barrier_semaphore()
    pl.semaphore_signal(barrier, inc=1, device_id={"tensor": 1 - side}, device_id_type=MESH)

    @pl.loop(1, n)
    def _(k):
        pl.semaphore_signal(barrier, inc=1, device_id={"head": lax.rem(me + k, n)}, device_id_type=MESH)

    loads[0].wait()
    loads[1].wait()

    @pl.loop(0, graphs)
    def _(g):
        rows = pl.ds(pl.multiple_of(g * part_rows, part_rows), part_rows)
        for h in range(heads):
            cols = slice(h * HD, (h + 1) * HD)
            kv_pack[g * heads + h, :, :HD] = k_ref[rows, cols]
            kv_pack[g * heads + h, :, HD:] = v_ref[rows, cols]

    loads[2].wait()
    pl.semaphore_wait(barrier, n)
    pair = pltpu.make_async_remote_copy(
        src_ref=go_ref, dst_ref=grad_s, send_sem=pair_sem.at[0], recv_sem=pair_sem.at[1],
        device_id={"tensor": 1 - side}, device_id_type=MESH,
    )
    pair.start()

    def copy_to(which, pack, land, peer, slot):
        return pltpu.make_async_remote_copy(
            src_ref=pack.at[peer], dst_ref=land.at[slot],
            send_sem=send_sem.at[which, peer], recv_sem=recv_sem.at[which, slot],
            device_id={"head": peer}, device_id_type=MESH,
        )

    far_count = n // 2

    def send(which, pack, land, k):
        copy_to(which, pack, land, across(me, k, n), me).start()

    def send_near(which, pack, land):
        @pl.loop(1, far_count)
        def _(k):
            send(which, pack, land, k)

    @pl.loop(far_count, n)
    def _(k):
        send(0, kv_pack, kv_in, k)

    send_near(0, kv_pack, kv_in)
    loads[3].wait()
    loads[4].wait()
    loads[5].wait()
    near = pl.ds(pl.multiple_of(side * width, width), width)
    far = pl.ds(pl.multiple_of((1 - side) * width, width), width)
    attn_s[...] = lax.dot_general(go_ref[...], w_ref[:, near], NT, preferred_element_type=jnp.float32)
    pair.wait()
    attn_s[...] += lax.dot_general(grad_s[...], w_ref[:, far], NT, preferred_element_type=jnp.float32)

    @pl.loop(0, graphs)
    def _(g):
        rows = pl.ds(pl.multiple_of(g * part_rows, part_rows), part_rows)
        for h in range(heads):
            cols = slice(h * HD, (h + 1) * HD)
            qg_pack[g * heads + h, :, :HD] = q_ref[rows, cols]
            qg_pack[g * heads + h, :, HD:] = attn_s[rows, cols].astype(jnp.bfloat16)

    early = far_count // 2

    @pl.loop(far_count, far_count + early)
    def _(k):
        send(1, qg_pack, qg_in, k)

    send_near(1, qg_pack, qg_in)

    def gather(which, pack, land, out):
        span = BS * min(WIDE, nodes // BS)
        land[me] = pack[me]
        acc_s[...] = jnp.zeros_like(acc_s)

        @pl.loop(0, n)
        def _(k):
            source = across(me, k, n)

            @pl.when(k >= far_count)
            def _():
                copy_to(which, pack, land, source, me).wait_send()
                if which == 0:
                    @pl.when(k + early < n)
                    def _():
                        send(1, qg_pack, qg_in, k + early)

            @pl.when(k > 0)
            def _():
                copy_to(which, pack, land, source, source).wait_recv()

            row = row_ref[source]
            block = marks(row // BS, (PACKED, part_rows))
            ids = lax.broadcasted_iota(jnp.int32, (BS, part_rows), 0)
            same = jnp.where(ids == row % BS, 1.0, 0.0).astype(jnp.bfloat16)
            chunk = land[source]

            @pl.loop(0, nodes // span)
            def _(t):
                hot = []
                for c in range(span // BS):
                    here = block == marks(jnp.full((1, 1), t * (span // BS) + c), (PACKED, part_rows))
                    hot += [jnp.where(here, same[r:r + PACKED], jnp.zeros_like(block)) for r in range(0, BS, PACKED)]
                rows = pl.ds(pl.multiple_of(t * span, span), span)
                acc_s[rows] += dot(jnp.concatenate(hot, axis=0), chunk)

        out[...] = acc_s[...].astype(jnp.bfloat16)

    gather(0, kv_pack, kv_in, kv_out)
    gather(1, qg_pack, qg_in, qg_out)

    @pl.loop(1, far_count)
    def _(k):
        peer = across(me, k, n)
        copy_to(0, kv_pack, kv_in, peer, me).wait_send()
        copy_to(1, qg_pack, qg_in, peer, me).wait_send()


def spreading(order, query, keys_in, values_in, grad_out, w_out, n):
    nodes = order.shape[0]
    part_rows = nodes // n
    vmem = pl.BlockSpec(memory_space=pltpu.VMEM)
    chunks = pltpu.VMEM((n, part_rows, 2 * HD), jnp.bfloat16)
    half = jax.ShapeDtypeStruct((nodes, 2 * HD), jnp.bfloat16)
    return pl.pallas_call(
        spread,
        out_shape=(half, half),
        in_specs=[pl.BlockSpec(memory_space=pltpu.HBM)] * 6,
        out_specs=(vmem, vmem),
        scratch_shapes=[
            pltpu.VMEM((n, 1, part_rows), jnp.int32),
            pltpu.VMEM(query.shape, jnp.bfloat16),
            pltpu.VMEM(query.shape, jnp.bfloat16),
            pltpu.VMEM(query.shape, jnp.bfloat16),
            pltpu.VMEM(grad_out.shape, jnp.bfloat16),
            pltpu.VMEM(w_out.shape, jnp.bfloat16),
            pltpu.SemaphoreType.DMA((6,)),
            pltpu.VMEM(grad_out.shape, jnp.bfloat16),
            pltpu.VMEM(query.shape, jnp.float32),
            chunks, chunks, chunks, chunks,
            pltpu.VMEM((nodes, 2 * HD), jnp.float32),
            pltpu.SemaphoreType.DMA((2,)),
            pltpu.SemaphoreType.DMA((2, n)),
            pltpu.SemaphoreType.DMA((2, n)),
        ],
        compiler_params=pltpu.CompilerParams(
            vmem_limit_bytes=SPREAD_BYTES, collective_id=0, has_side_effects=True
        ),
        name="spread",
    )(*in_hbm(order.reshape(n, 1, part_rows), query, keys_in, values_in, grad_out, w_out))


def attend(block_ref, count_ref, qg_ref, kv_ref, out_ref, kt_s, qg_s, dkv_s, dqt_s, e_s, d_s, top_s, sum_s, dot_s, task, trips):
    block_count = kv_ref.shape[0]
    slots = block_ref.shape[0]
    groups = top_s.shape[1]
    span = task.shape[0] // ROUNDS
    share = block_count // ROUNDS
    scale = HD ** (-0.5)
    low = lax.broadcasted_iota(jnp.int32, (BS, 2 * HD), 1) < HD

    width = 4

    def ready(i, t):
        for v in range(width):
            b = i * width + v
            count = count_ref[b]
            for g in range(slots // 2):
                on = (2 * g + 1 < count).astype(jnp.int32)
                task[t] = b + (g << 8) + (on << 12) + (block_ref[2 * g, 0, b] << 16) + (block_ref[2 * g + 1, 0, b] << 24)
                t = t + (2 * g < count).astype(jnp.int32)
            qg = qg_ref[b].astype(jnp.float32)
            qg_s[b, :BS] = jnp.where(low, qg * scale, 0.0).astype(jnp.bfloat16)
            qg_s[b, BS:] = jnp.where(low, 0.0, qg).astype(jnp.bfloat16)
            kt_s[b] = (kv_ref[b].astype(jnp.float32).T[:HD] * scale).astype(jnp.bfloat16)
            dkv_s[b] = jnp.zeros((BS, 2 * HD), jnp.float32)
            dqt_s[b] = jnp.zeros((HD, BS), jnp.float32)
        return t

    for r in range(ROUNDS):
        total = lax.fori_loop(r * share // width, (r + 1) * share // width, ready, r * span)
        for u in range(UNROLL - 1):
            task[total + u] = block_count + (1 << 12)
        trips[r] = (total - r * span + UNROLL - 1) // UNROLL

    def read(r, t):
        code = task[r * span + t]
        return code & 255, (code >> 8) & 15, (code >> 12) & 1, [(code >> 16) & 255, (code >> 24) & 255]

    qg_s[block_count] = jnp.zeros((2 * BS, 2 * HD), jnp.bfloat16)
    top_s[...] = jnp.full(top_s.shape, -1e30, jnp.float32)
    sum_s[...] = jnp.zeros(sum_s.shape, jnp.float32)
    dot_s[...] = jnp.zeros(dot_s.shape, jnp.float32)

    def forward(r, t):
        b, g, on, c = read(r, t)
        qg = qg_s[b]
        sd = [lax.dot_general(kv_ref[c[k]], qg, NT, preferred_element_type=jnp.float32) for k in (0, 1)]
        s = [sd[0][:, :BS], jnp.where(on > 0, sd[1][:, :BS], -jnp.inf)]
        top = jnp.max(jnp.maximum(s[0], s[1]), axis=0, keepdims=True)
        e = [jnp.exp(x - top) for x in s]
        d = [x[:, BS:] for x in sd]
        for k in (0, 1):
            e_s[2 * t + k] = e[k]
            d_s[2 * t + k] = d[k]
        row = pl.ds(b, 1)
        top_s[r, g, row] = top
        sum_s[r, g, row] = jnp.sum(e[0] + e[1], axis=0, keepdims=True)
        dot_s[r, g, row] = jnp.sum(e[0] * d[0] + e[1] * d[1], axis=0, keepdims=True)

    def backward(r, t):
        b, g, _, c = read(r, t)
        qg = qg_s[b]
        row = pl.ds(b, 1)
        factor = top_s[r, g, row]
        delta = sum_s[r, 0, row]
        ds, upd = [], []
        for k in (0, 1):
            p = e_s[2 * t + k] * factor
            ds.append((p * (d_s[2 * t + k] - delta)).astype(jnp.bfloat16))
            upd.append(dot(jnp.concatenate((ds[k], p.astype(jnp.bfloat16)), axis=1), qg))
        kt = jnp.concatenate((kt_s[c[0]], kt_s[c[1]]), axis=1)
        return b, c, upd, dot(kt, jnp.concatenate(ds, axis=0))

    @pl.loop(0, ROUNDS)
    def _(r):
        @pl.loop(0, trips[r])
        def _(i):
            for u in range(UNROLL):
                forward(r, i * UNROLL + u)

        tops = [top_s[r, g] for g in range(groups)]
        top = tops[0]
        for x in tops[1:]:
            top = jnp.maximum(top, x)
        part = [jnp.exp(x - top) for x in tops]
        inv = 1.0 / sum(part[g] * sum_s[r, g] for g in range(groups))
        delta = sum(part[g] * dot_s[r, g] for g in range(groups)) * inv
        for g in range(groups):
            top_s[r, g] = part[g] * inv
        sum_s[r, 0] = delta

        @pl.loop(0, trips[r])
        def _(i):
            done = [backward(r, i * UNROLL + u) for u in range(UNROLL)]
            for b, c, upd, dqt in done:
                for k in (0, 1):
                    dkv_s[c[k]] += upd[k]
                dqt_s[b] += dqt

    @pl.loop(0, block_count, unroll=4)
    def _(b):
        rows = pl.ds(pl.multiple_of(b * BS, BS), BS)
        dqt = dqt_s[b]
        out_ref[rows, :2 * HD] = dkv_s[b].astype(jnp.bfloat16)
        out_ref[rows, 2 * HD:] = jnp.concatenate((dqt, dqt), axis=0).T.astype(jnp.bfloat16)

def attention(qg, kv, block_col, count_row):
    nodes = qg.shape[0]
    block_count = nodes // BS
    slots = block_col.shape[0]
    groups = (slots + 1) // 2
    tasks = block_count // ROUNDS * groups + UNROLL
    rows = block_count + 8
    vmem = pl.BlockSpec(memory_space=pltpu.VMEM)
    smem = pl.BlockSpec(memory_space=pltpu.SMEM)
    return pl.pallas_call(
        attend,
        out_shape=jax.ShapeDtypeStruct((nodes, 4 * HD), jnp.bfloat16),
        in_specs=[smem, smem, vmem, vmem],
        out_specs=vmem,
        scratch_shapes=[
            pltpu.VMEM((block_count, HD, BS), jnp.bfloat16),
            pltpu.VMEM((block_count + 1, 2 * BS, 2 * HD), jnp.bfloat16),
            pltpu.VMEM((block_count, BS, 2 * HD), jnp.float32),
            pltpu.VMEM((block_count + 1, HD, BS), jnp.float32),
            pltpu.VMEM((2 * tasks, BS, BS), jnp.float32),
            pltpu.VMEM((2 * tasks, BS, BS), jnp.float32),
            pltpu.VMEM((ROUNDS, groups, rows, BS), jnp.float32),
            pltpu.VMEM((ROUNDS, groups, rows, BS), jnp.float32),
            pltpu.VMEM((ROUNDS, groups, rows, BS), jnp.float32),
            pltpu.SMEM((ROUNDS * tasks,), jnp.int32),
            pltpu.SMEM((ROUNDS,), jnp.int32),
        ],
        compiler_params=pltpu.CompilerParams(vmem_limit_bytes=ATTEND_BYTES),
        name="attend",
    )(block_col, count_row, qg.reshape(block_count, BS, 2 * HD), kv.reshape(block_count, BS, 2 * HD))


def collect(row_ref, g_ref, wq_hbm, wk_hbm, wv_hbm, out_ref,
            wq_ref, wk_ref, wv_ref, load_sem, block_s, spot_s, pack, land, w_s, acc_s, give_s, got_s, pair_sem, send_sem, recv_sem):
    n, out_rows, _ = land.shape
    half = out_rows // 3
    graphs = out_ref.shape[0]
    heads = n // graphs
    nodes = g_ref.shape[0]
    me = lax.axis_index("head")
    side = lax.axis_index("tensor")
    loads = [
        pltpu.make_async_copy(src, dst, load_sem.at[at])
        for at, (src, dst) in enumerate(((wq_hbm, wq_ref), (wk_hbm, wk_ref), (wv_hbm, wv_ref)))
    ]
    for load in loads:
        load.start()
    barrier = pltpu.get_barrier_semaphore()
    pl.semaphore_signal(barrier, inc=1, device_id={"tensor": 1 - side}, device_id_type=MESH)

    @pl.loop(1, n)
    def _(k):
        pl.semaphore_signal(barrier, inc=1, device_id={"head": lax.rem(me + k, n)}, device_id_type=MESH)

    order = row_ref[:, 0, :]
    block_s[...] = (order // BS).astype(jnp.float32).T
    spot_s[...] = (order % BS).astype(jnp.float32).T

    def make(peer, into):
        mine = lax.broadcasted_iota(jnp.int32, (2 * half, n), 1) == peer
        block = marks(jnp.sum(jnp.where(mine, block_s[...], 0.0), axis=1, keepdims=True), (2 * half, BS))
        spot = jnp.sum(jnp.where(mine, spot_s[...], 0.0), axis=1, keepdims=True)
        ids = lax.broadcasted_iota(jnp.int32, (2 * half, BS), 1).astype(jnp.float32)
        same = jnp.where(ids == spot, 1.0, 0.0).astype(jnp.bfloat16)
        hot = [jnp.where(block == jnp.bfloat16(c), same, jnp.zeros_like(same)) for c in range(nodes // BS)]
        got = dot(jnp.concatenate(hot, axis=1), g_ref[...])
        into[:2 * half] = got[:, :2 * HD].astype(jnp.bfloat16)
        low = lax.broadcasted_iota(jnp.int32, (half, 2 * HD), 1) < HD
        into[2 * half:] = jnp.where(low, got[:half, 2 * HD:], got[half:, 2 * HD:]).astype(jnp.bfloat16)

    def copy_to(peer, slot):
        return pltpu.make_async_remote_copy(
            src_ref=pack.at[peer], dst_ref=land.at[slot],
            send_sem=send_sem.at[peer], recv_sem=recv_sem.at[slot],
            device_id={"head": peer}, device_id_type=MESH,
        )

    far_count = n // 2

    def serve(peer):
        make(peer, pack.at[peer])
        copy_to(peer, me).start()

    first = across(me, far_count, n)
    make(first, pack.at[first])
    pl.semaphore_wait(barrier, n)
    copy_to(first, me).start()

    ahead = far_count - far_count // 4

    @pl.loop(far_count + 1, far_count + ahead)
    def _(k):
        serve(across(me, k, n))

    @pl.loop(1, far_count)
    def _(k):
        serve(across(me, k, n))

    @pl.loop(far_count + ahead, n)
    def _(k):
        make(across(me, k, n), pack.at[across(me, k, n)])

    make(me, land.at[me])
    for load in loads:
        load.wait()
    for h in range(heads):
        cols = slice(h * HD, (h + 1) * HD)
        for part in range(2):
            w_s[h, part, :, :HD] = wk_ref[:, cols]
            w_s[h, part, :, HD:2 * HD] = wv_ref[:, cols]
            w_s[h, part, :, (2 + part) * HD:(3 + part) * HD] = wq_ref[:, cols]
            w_s[h, part, :, (3 - part) * HD:(4 - part) * HD] = jnp.zeros((w_s.shape[2], HD), jnp.bfloat16)
    acc_s[...] = jnp.zeros_like(acc_s)

    def project(slot, part):
        rows = pl.ds(pl.multiple_of(part * half, half), half)
        left = jnp.concatenate((land[slot, rows], land[slot, 2 * half:]), axis=1)
        acc_s[slot // heads, part] += lax.dot_general(
            left, w_s[lax.rem(slot, heads), part], NT, preferred_element_type=jnp.float32
        )

    @pl.loop(0, n - 1)
    def _(k):
        source = across(me, k, n)

        @pl.when(k >= far_count)
        def _():
            copy_to(source, me).wait_send()

            @pl.when(k + ahead < n)
            def _():
                copy_to(across(me, k + ahead, n), me).start()

        @pl.when(k > 0)
        def _():
            copy_to(source, source).wait_recv()

        for part in range(2):
            project(source, part)

    last = across(me, n - 1, n)
    copy_to(last, last).wait_recv()
    project(last, 1 - side)
    give_s[...] = acc_s[:, 1 - side].astype(jnp.bfloat16)
    pair = pltpu.make_async_remote_copy(
        src_ref=give_s, dst_ref=got_s, send_sem=pair_sem.at[0], recv_sem=pair_sem.at[1],
        device_id={"tensor": 1 - side}, device_id_type=MESH,
    )
    pair.start()
    project(last, side)
    pair.wait()
    out_ref[...] = (acc_s[:, side] + got_s[...].astype(jnp.float32)).astype(jnp.bfloat16)

    copy_to(last, me).wait_send()

    @pl.loop(1, far_count)
    def _(k):
        copy_to(across(me, k, n), me).wait_send()


def collecting(order, grads, w_query, w_key, w_value, graphs, n):
    nodes = order.shape[0]
    part_rows = nodes // n
    half = part_rows // 2
    full, width = w_query.shape
    heads = width // HD
    vmem = pl.BlockSpec(memory_space=pltpu.VMEM)
    chunks = pltpu.VMEM((n, part_rows * 3 // 2, 2 * HD), jnp.bfloat16)
    result = (graphs, half, full)
    return pl.pallas_call(
        collect,
        out_shape=jax.ShapeDtypeStruct(result, jnp.bfloat16),
        in_specs=[vmem] * 2 + [pl.BlockSpec(memory_space=pltpu.HBM)] * 3,
        out_specs=vmem,
        scratch_shapes=[
            pltpu.VMEM(w_query.shape, jnp.bfloat16),
            pltpu.VMEM(w_query.shape, jnp.bfloat16),
            pltpu.VMEM(w_query.shape, jnp.bfloat16),
            pltpu.SemaphoreType.DMA((3,)),
            pltpu.VMEM((part_rows, n), jnp.float32),
            pltpu.VMEM((part_rows, n), jnp.float32),
            chunks, chunks,
            pltpu.VMEM((heads, 2, full, 4 * HD), jnp.bfloat16),
            pltpu.VMEM((graphs, 2, half, full), jnp.float32),
            pltpu.VMEM(result, jnp.bfloat16),
            pltpu.VMEM(result, jnp.bfloat16),
            pltpu.SemaphoreType.DMA((2,)),
            pltpu.SemaphoreType.DMA((n,)),
            pltpu.SemaphoreType.DMA((n,)),
        ],
        compiler_params=pltpu.CompilerParams(
            vmem_limit_bytes=COLLECT_BYTES, collective_id=1, has_side_effects=True
        ),
        name="collect",
    )(order.reshape(n, 1, part_rows), grads, *in_hbm(w_query, w_key, w_value))


def on_device(
    query, keys_in, values_in, grad_out, w_out, w_query, w_key, w_value, perm, blocks, counts
):
    local_rows, half_width = query.shape
    graphs, nodes = perm.shape
    half_heads = half_width // HD
    part_rows = local_rows // graphs
    n = nodes // part_rows
    graph = lax.axis_index("head") // half_heads
    order = lax.dynamic_index_in_dim(perm, graph, 0, keepdims=False)
    block_row = lax.dynamic_index_in_dim(blocks.transpose(2, 0, 1), graph, 1)
    count_row = lax.dynamic_index_in_dim(counts, graph, 0, keepdims=False)
    by_graph = [
        member.reshape(part_rows, graphs, half_width).transpose(1, 0, 2).reshape(local_rows, half_width)
        for member in (query, keys_in, values_in, grad_out)
    ]
    qg, kv = spreading(order, *by_graph, w_out, n)
    grads = attention(qg, kv, block_row, count_row)
    total = collecting(order, grads, w_query, w_key, w_value, graphs, n)
    return total.transpose(1, 0, 2).reshape(local_rows // 2, -1)


def solution(mesh):
    return jax.shard_map(
        on_device,
        mesh=mesh,
        in_specs=(
            P(("groups", "head"), "tensor"),
            P(("groups", "head"), "tensor"),
            P(("groups", "head"), "tensor"),
            P(("groups", "head"), "tensor"),
            P("tensor", None),
            P(None, "tensor"),
            P(None, "tensor"),
            P(None, "tensor"),
            P("groups", None),
            P("groups", None, None),
            P("groups", None),
        ),
        out_specs=P(("groups", "head", "tensor"), None),
        check_vma=False,
    )
```

```python
import jax
import jax.numpy as jnp
from jax import lax
from jax.experimental import pallas as pl
from jax.experimental.pallas import tpu as pltpu
from jax.sharding import PartitionSpec as P

HD = 64
BS = 128
NT = (((1,), (1,)), ((), ()))
UNROLL = 16
ROUNDS = 2
PACKED = 16
WIDE = 32
SPREAD_BYTES = 25165824
ATTEND_BYTES = 44040192
COLLECT_BYTES = 33554432
MESH = pl.DeviceIdType.MESH


def dot(a, b):
    return jnp.dot(a, b, preferred_element_type=jnp.float32)


def in_hbm(*arrays):
    return [pltpu.with_memory_space_constraint(x, pltpu.HBM) for x in arrays]


def marks(values, shape):
    return jnp.broadcast_to(values.astype(jnp.float32), shape).astype(jnp.bfloat16)


def across(i, k, n):
    out = 0
    bit = 1
    while bit < n:
        a, b = lax.rem(i // bit, 2), lax.rem(k // bit, 2)
        out += (a + b - 2 * a * b) * bit
        bit *= 2
    return out


def spread(row_hbm, q_hbm, k_hbm, v_hbm, go_hbm, w_hbm, qg_out, kv_out,
           row_ref, q_ref, k_ref, v_ref, go_ref, w_ref, load_sem, grad_s, attn_s, kv_pack, qg_pack, kv_in, qg_in, acc_s, pair_sem, send_sem, recv_sem):
    n, part_rows, _ = kv_in.shape
    heads = q_ref.shape[1] // HD
    graphs = n // heads
    nodes = n * part_rows
    me = lax.axis_index("head")
    side = lax.axis_index("tensor")
    width = go_ref.shape[1]
    loads = [
        pltpu.make_async_copy(src, dst, load_sem.at[at])
        for at, (src, dst) in enumerate(
            ((k_hbm, k_ref), (v_hbm, v_ref), (go_hbm, go_ref), (q_hbm, q_ref), (w_hbm, w_ref), (row_hbm, row_ref))
        )
    ]
    for load in loads:
        load.start()
    barrier = pltpu.get_barrier_semaphore()
    pl.semaphore_signal(barrier, inc=1, device_id={"tensor": 1 - side}, device_id_type=MESH)

    @pl.loop(1, n)
    def _(k):
        pl.semaphore_signal(barrier, inc=1, device_id={"head": lax.rem(me + k, n)}, device_id_type=MESH)

    loads[0].wait()
    loads[1].wait()

    @pl.loop(0, graphs)
    def _(g):
        rows = pl.ds(pl.multiple_of(g * part_rows, part_rows), part_rows)
        for h in range(heads):
            cols = slice(h * HD, (h + 1) * HD)
            kv_pack[g * heads + h, :, :HD] = k_ref[rows, cols]
            kv_pack[g * heads + h, :, HD:] = v_ref[rows, cols]

    loads[2].wait()
    pl.semaphore_wait(barrier, n)
    pair = pltpu.make_async_remote_copy(
        src_ref=go_ref, dst_ref=grad_s, send_sem=pair_sem.at[0], recv_sem=pair_sem.at[1],
        device_id={"tensor": 1 - side}, device_id_type=MESH,
    )
    pair.start()

    def copy_to(which, pack, land, peer, slot):
        return pltpu.make_async_remote_copy(
            src_ref=pack.at[peer], dst_ref=land.at[slot],
            send_sem=send_sem.at[which, peer], recv_sem=recv_sem.at[which, slot],
            device_id={"head": peer}, device_id_type=MESH,
        )

    far_count = n // 2

    def send(which, pack, land, k):
        copy_to(which, pack, land, across(me, k, n), me).start()

    def send_near(which, pack, land):
        @pl.loop(1, far_count)
        def _(k):
            send(which, pack, land, k)

    @pl.loop(far_count, n)
    def _(k):
        send(0, kv_pack, kv_in, k)

    send_near(0, kv_pack, kv_in)
    loads[3].wait()
    loads[4].wait()
    loads[5].wait()
    near = pl.ds(pl.multiple_of(side * width, width), width)
    far = pl.ds(pl.multiple_of((1 - side) * width, width), width)
    attn_s[...] = lax.dot_general(go_ref[...], w_ref[:, near], NT, preferred_element_type=jnp.float32)
    pair.wait()
    attn_s[...] += lax.dot_general(grad_s[...], w_ref[:, far], NT, preferred_element_type=jnp.float32)

    @pl.loop(0, graphs)
    def _(g):
        rows = pl.ds(pl.multiple_of(g * part_rows, part_rows), part_rows)
        for h in range(heads):
            cols = slice(h * HD, (h + 1) * HD)
            qg_pack[g * heads + h, :, :HD] = q_ref[rows, cols]
            qg_pack[g * heads + h, :, HD:] = attn_s[rows, cols].astype(jnp.bfloat16)

    early = far_count // 2

    @pl.loop(far_count, far_count + early)
    def _(k):
        send(1, qg_pack, qg_in, k)

    send_near(1, qg_pack, qg_in)

    def gather(which, pack, land, out):
        span = BS * min(WIDE, nodes // BS)
        land[me] = pack[me]
        acc_s[...] = jnp.zeros_like(acc_s)

        @pl.loop(0, n)
        def _(k):
            source = across(me, k, n)

            @pl.when(k >= far_count)
            def _():
                copy_to(which, pack, land, source, me).wait_send()
                if which == 0:
                    @pl.when(k + early < n)
                    def _():
                        send(1, qg_pack, qg_in, k + early)

            @pl.when(k > 0)
            def _():
                copy_to(which, pack, land, source, source).wait_recv()

            row = row_ref[source]
            block = marks(row // BS, (PACKED, part_rows))
            ids = lax.broadcasted_iota(jnp.int32, (BS, part_rows), 0)
            same = jnp.where(ids == row % BS, 1.0, 0.0).astype(jnp.bfloat16)
            chunk = land[source]

            @pl.loop(0, nodes // span)
            def _(t):
                hot = []
                for c in range(span // BS):
                    here = block == marks(jnp.full((1, 1), t * (span // BS) + c), (PACKED, part_rows))
                    hot += [jnp.where(here, same[r:r + PACKED], jnp.zeros_like(block)) for r in range(0, BS, PACKED)]
                rows = pl.ds(pl.multiple_of(t * span, span), span)
                acc_s[rows] += dot(jnp.concatenate(hot, axis=0), chunk)

        out[...] = acc_s[...].astype(jnp.bfloat16)

    gather(0, kv_pack, kv_in, kv_out)
    gather(1, qg_pack, qg_in, qg_out)

    @pl.loop(1, far_count)
    def _(k):
        peer = across(me, k, n)
        copy_to(0, kv_pack, kv_in, peer, me).wait_send()
        copy_to(1, qg_pack, qg_in, peer, me).wait_send()


def spreading(order, query, keys_in, values_in, grad_out, w_out, n):
    nodes = order.shape[0]
    part_rows = nodes // n
    vmem = pl.BlockSpec(memory_space=pltpu.VMEM)
    chunks = pltpu.VMEM((n, part_rows, 2 * HD), jnp.bfloat16)
    half = jax.ShapeDtypeStruct((nodes, 2 * HD), jnp.bfloat16)
    return pl.pallas_call(
        spread,
        out_shape=(half, half),
        in_specs=[pl.BlockSpec(memory_space=pltpu.HBM)] * 6,
        out_specs=(vmem, vmem),
        scratch_shapes=[
            pltpu.VMEM((n, 1, part_rows), jnp.int32),
            pltpu.VMEM(query.shape, jnp.bfloat16),
            pltpu.VMEM(query.shape, jnp.bfloat16),
            pltpu.VMEM(query.shape, jnp.bfloat16),
            pltpu.VMEM(grad_out.shape, jnp.bfloat16),
            pltpu.VMEM(w_out.shape, jnp.bfloat16),
            pltpu.SemaphoreType.DMA((6,)),
            pltpu.VMEM(grad_out.shape, jnp.bfloat16),
            pltpu.VMEM(query.shape, jnp.float32),
            chunks, chunks, chunks, chunks,
            pltpu.VMEM((nodes, 2 * HD), jnp.float32),
            pltpu.SemaphoreType.DMA((2,)),
            pltpu.SemaphoreType.DMA((2, n)),
            pltpu.SemaphoreType.DMA((2, n)),
        ],
        compiler_params=pltpu.CompilerParams(
            vmem_limit_bytes=SPREAD_BYTES, collective_id=0, has_side_effects=True
        ),
        name="spread",
    )(*in_hbm(order.reshape(n, 1, part_rows), query, keys_in, values_in, grad_out, w_out))


def attend(block_ref, count_ref, qg_ref, kv_ref, out_ref, kt_s, qg_s, dkv_s, dqt_s, e_s, d_s, top_s, sum_s, dot_s, task, trips):
    block_count = kv_ref.shape[0]
    slots = block_ref.shape[0]
    groups = top_s.shape[1]
    span = task.shape[0] // ROUNDS
    share = block_count // ROUNDS
    scale = HD ** (-0.5)
    low = lax.broadcasted_iota(jnp.int32, (BS, 2 * HD), 1) < HD

    width = 8

    def ready(i, t):
        for v in range(width):
            b = i * width + v
            count = count_ref[b]
            for g in range(slots // 2):
                on = (2 * g + 1 < count).astype(jnp.int32)
                task[t] = b + (g << 8) + (on << 12) + (block_ref[2 * g, 0, b] << 16) + (block_ref[2 * g + 1, 0, b] << 24)
                t = t + (2 * g < count).astype(jnp.int32)
            qg = qg_ref[b].astype(jnp.float32)
            qg_s[b, :BS] = jnp.where(low, qg * scale, 0.0).astype(jnp.bfloat16)
            qg_s[b, BS:] = jnp.where(low, 0.0, qg).astype(jnp.bfloat16)
            kt_s[b] = (kv_ref[b].astype(jnp.float32).T[:HD] * scale).astype(jnp.bfloat16)
            dkv_s[b] = jnp.zeros((BS, 2 * HD), jnp.float32)
            dqt_s[b] = jnp.zeros((HD, BS), jnp.float32)
        return t

    for r in range(ROUNDS):
        total = lax.fori_loop(r * share // width, (r + 1) * share // width, ready, r * span)
        for u in range(UNROLL - 1):
            task[total + u] = block_count + (1 << 12)
        trips[r] = (total - r * span + UNROLL - 1) // UNROLL

    def read(r, t):
        code = task[r * span + t]
        return code & 255, (code >> 8) & 15, (code >> 12) & 1, [(code >> 16) & 255, (code >> 24) & 255]

    qg_s[block_count] = jnp.zeros((2 * BS, 2 * HD), jnp.bfloat16)
    top_s[...] = jnp.full(top_s.shape, -1e30, jnp.float32)
    sum_s[...] = jnp.zeros(sum_s.shape, jnp.float32)
    dot_s[...] = jnp.zeros(dot_s.shape, jnp.float32)

    def forward(r, t):
        b, g, on, c = read(r, t)
        qg = qg_s[b]
        sd = [lax.dot_general(kv_ref[c[k]], qg, NT, preferred_element_type=jnp.float32) for k in (0, 1)]
        s = [sd[0][:, :BS], jnp.where(on > 0, sd[1][:, :BS], -jnp.inf)]
        top = jnp.max(jnp.maximum(s[0], s[1]), axis=0, keepdims=True)
        e = [jnp.exp(x - top) for x in s]
        d = [x[:, BS:] for x in sd]
        for k in (0, 1):
            e_s[2 * t + k] = e[k]
            d_s[2 * t + k] = d[k]
        row = pl.ds(b, 1)
        top_s[r, g, row] = top
        sum_s[r, g, row] = jnp.sum(e[0] + e[1], axis=0, keepdims=True)
        dot_s[r, g, row] = jnp.sum(e[0] * d[0] + e[1] * d[1], axis=0, keepdims=True)

    def backward(r, t):
        b, g, _, c = read(r, t)
        qg = qg_s[b]
        row = pl.ds(b, 1)
        factor = top_s[r, g, row]
        delta = sum_s[r, 0, row]
        ds, upd = [], []
        for k in (0, 1):
            p = e_s[2 * t + k] * factor
            ds.append((p * (d_s[2 * t + k] - delta)).astype(jnp.bfloat16))
            upd.append(dot(jnp.concatenate((ds[k], p.astype(jnp.bfloat16)), axis=1), qg))
        kt = jnp.concatenate((kt_s[c[0]], kt_s[c[1]]), axis=1)
        return b, c, upd, dot(kt, jnp.concatenate(ds, axis=0))

    @pl.loop(0, ROUNDS)
    def _(r):
        @pl.loop(0, trips[r])
        def _(i):
            for u in range(UNROLL):
                forward(r, i * UNROLL + u)

        tops = [top_s[r, g] for g in range(groups)]
        top = tops[0]
        for x in tops[1:]:
            top = jnp.maximum(top, x)
        part = [jnp.exp(x - top) for x in tops]
        inv = 1.0 / sum(part[g] * sum_s[r, g] for g in range(groups))
        delta = sum(part[g] * dot_s[r, g] for g in range(groups)) * inv
        for g in range(groups):
            top_s[r, g] = part[g] * inv
        sum_s[r, 0] = delta

        @pl.loop(0, trips[r])
        def _(i):
            done = [backward(r, i * UNROLL + u) for u in range(UNROLL)]
            for b, c, upd, dqt in done:
                for k in (0, 1):
                    dkv_s[c[k]] += upd[k]
                dqt_s[b] += dqt

    @pl.loop(0, block_count, unroll=8)
    def _(b):
        rows = pl.ds(pl.multiple_of(b * BS, BS), BS)
        dqt = dqt_s[b]
        out_ref[rows, :2 * HD] = dkv_s[b].astype(jnp.bfloat16)
        out_ref[rows, 2 * HD:] = jnp.concatenate((dqt, dqt), axis=0).T.astype(jnp.bfloat16)

def attention(qg, kv, block_col, count_row):
    nodes = qg.shape[0]
    block_count = nodes // BS
    slots = block_col.shape[0]
    groups = (slots + 1) // 2
    tasks = block_count // ROUNDS * groups + UNROLL
    rows = block_count + 8
    vmem = pl.BlockSpec(memory_space=pltpu.VMEM)
    smem = pl.BlockSpec(memory_space=pltpu.SMEM)
    return pl.pallas_call(
        attend,
        out_shape=jax.ShapeDtypeStruct((nodes, 4 * HD), jnp.bfloat16),
        in_specs=[smem, smem, vmem, vmem],
        out_specs=vmem,
        scratch_shapes=[
            pltpu.VMEM((block_count, HD, BS), jnp.bfloat16),
            pltpu.VMEM((block_count + 1, 2 * BS, 2 * HD), jnp.bfloat16),
            pltpu.VMEM((block_count, BS, 2 * HD), jnp.float32),
            pltpu.VMEM((block_count + 1, HD, BS), jnp.float32),
            pltpu.VMEM((2 * tasks, BS, BS), jnp.float32),
            pltpu.VMEM((2 * tasks, BS, BS), jnp.float32),
            pltpu.VMEM((ROUNDS, groups, rows, BS), jnp.float32),
            pltpu.VMEM((ROUNDS, groups, rows, BS), jnp.float32),
            pltpu.VMEM((ROUNDS, groups, rows, BS), jnp.float32),
            pltpu.SMEM((ROUNDS * tasks,), jnp.int32),
            pltpu.SMEM((ROUNDS,), jnp.int32),
        ],
        compiler_params=pltpu.CompilerParams(vmem_limit_bytes=ATTEND_BYTES),
        name="attend",
    )(block_col, count_row, qg.reshape(block_count, BS, 2 * HD), kv.reshape(block_count, BS, 2 * HD))


def collect(row_ref, g_ref, wq_hbm, wk_hbm, wv_hbm, out_ref,
            wq_ref, wk_ref, wv_ref, load_sem, block_s, spot_s, pack, land, w_s, acc_s, give_s, got_s, pair_sem, send_sem, recv_sem):
    n, out_rows, _ = land.shape
    half = out_rows // 3
    graphs = out_ref.shape[0]
    heads = n // graphs
    nodes = g_ref.shape[0]
    me = lax.axis_index("head")
    side = lax.axis_index("tensor")
    loads = [
        pltpu.make_async_copy(src, dst, load_sem.at[at])
        for at, (src, dst) in enumerate(((wq_hbm, wq_ref), (wk_hbm, wk_ref), (wv_hbm, wv_ref)))
    ]
    for load in loads:
        load.start()
    barrier = pltpu.get_barrier_semaphore()
    pl.semaphore_signal(barrier, inc=1, device_id={"tensor": 1 - side}, device_id_type=MESH)

    @pl.loop(1, n)
    def _(k):
        pl.semaphore_signal(barrier, inc=1, device_id={"head": lax.rem(me + k, n)}, device_id_type=MESH)

    order = row_ref[:, 0, :]
    block_s[...] = (order // BS).astype(jnp.float32).T
    spot_s[...] = (order % BS).astype(jnp.float32).T

    def make(peer, into):
        mine = lax.broadcasted_iota(jnp.int32, (2 * half, n), 1) == peer
        block = marks(jnp.sum(jnp.where(mine, block_s[...], 0.0), axis=1, keepdims=True), (2 * half, BS))
        spot = jnp.sum(jnp.where(mine, spot_s[...], 0.0), axis=1, keepdims=True)
        ids = lax.broadcasted_iota(jnp.int32, (2 * half, BS), 1).astype(jnp.float32)
        same = jnp.where(ids == spot, 1.0, 0.0).astype(jnp.bfloat16)
        hot = [jnp.where(block == jnp.bfloat16(c), same, jnp.zeros_like(same)) for c in range(nodes // BS)]
        got = dot(jnp.concatenate(hot, axis=1), g_ref[...])
        into[:2 * half] = got[:, :2 * HD].astype(jnp.bfloat16)
        low = lax.broadcasted_iota(jnp.int32, (half, 2 * HD), 1) < HD
        into[2 * half:] = jnp.where(low, got[:half, 2 * HD:], got[half:, 2 * HD:]).astype(jnp.bfloat16)

    def copy_to(peer, slot):
        return pltpu.make_async_remote_copy(
            src_ref=pack.at[peer], dst_ref=land.at[slot],
            send_sem=send_sem.at[peer], recv_sem=recv_sem.at[slot],
            device_id={"head": peer}, device_id_type=MESH,
        )

    far_count = n // 2

    def serve(peer):
        make(peer, pack.at[peer])
        copy_to(peer, me).start()

    first = across(me, far_count, n)
    make(first, pack.at[first])
    pl.semaphore_wait(barrier, n)
    copy_to(first, me).start()

    ahead = far_count - far_count // 4

    @pl.loop(far_count + 1, far_count + ahead)
    def _(k):
        serve(across(me, k, n))

    @pl.loop(1, far_count)
    def _(k):
        serve(across(me, k, n))

    @pl.loop(far_count + ahead, n)
    def _(k):
        make(across(me, k, n), pack.at[across(me, k, n)])

    make(me, land.at[me])
    for load in loads:
        load.wait()
    for h in range(heads):
        cols = slice(h * HD, (h + 1) * HD)
        for part in range(2):
            w_s[h, part, :, :HD] = wk_ref[:, cols]
            w_s[h, part, :, HD:2 * HD] = wv_ref[:, cols]
            w_s[h, part, :, (2 + part) * HD:(3 + part) * HD] = wq_ref[:, cols]
            w_s[h, part, :, (3 - part) * HD:(4 - part) * HD] = jnp.zeros((w_s.shape[2], HD), jnp.bfloat16)
    acc_s[...] = jnp.zeros_like(acc_s)

    def project(slot, part):
        rows = pl.ds(pl.multiple_of(part * half, half), half)
        left = jnp.concatenate((land[slot, rows], land[slot, 2 * half:]), axis=1)
        acc_s[slot // heads, part] += lax.dot_general(
            left, w_s[lax.rem(slot, heads), part], NT, preferred_element_type=jnp.float32
        )

    @pl.loop(0, n - 1)
    def _(k):
        source = across(me, k, n)

        @pl.when(k >= far_count)
        def _():
            copy_to(source, me).wait_send()

            @pl.when(k + ahead < n)
            def _():
                copy_to(across(me, k + ahead, n), me).start()

        @pl.when(k > 0)
        def _():
            copy_to(source, source).wait_recv()

        for part in range(2):
            project(source, part)

    last = across(me, n - 1, n)
    copy_to(last, last).wait_recv()
    project(last, 1 - side)
    give_s[...] = acc_s[:, 1 - side].astype(jnp.bfloat16)
    pair = pltpu.make_async_remote_copy(
        src_ref=give_s, dst_ref=got_s, send_sem=pair_sem.at[0], recv_sem=pair_sem.at[1],
        device_id={"tensor": 1 - side}, device_id_type=MESH,
    )
    pair.start()
    project(last, side)
    pair.wait()
    out_ref[...] = (acc_s[:, side] + got_s[...].astype(jnp.float32)).astype(jnp.bfloat16)

    copy_to(last, me).wait_send()

    @pl.loop(1, far_count)
    def _(k):
        copy_to(across(me, k, n), me).wait_send()


def collecting(order, grads, w_query, w_key, w_value, graphs, n):
    nodes = order.shape[0]
    part_rows = nodes // n
    half = part_rows // 2
    full, width = w_query.shape
    heads = width // HD
    vmem = pl.BlockSpec(memory_space=pltpu.VMEM)
    chunks = pltpu.VMEM((n, part_rows * 3 // 2, 2 * HD), jnp.bfloat16)
    result = (graphs, half, full)
    return pl.pallas_call(
        collect,
        out_shape=jax.ShapeDtypeStruct(result, jnp.bfloat16),
        in_specs=[vmem] * 2 + [pl.BlockSpec(memory_space=pltpu.HBM)] * 3,
        out_specs=vmem,
        scratch_shapes=[
            pltpu.VMEM(w_query.shape, jnp.bfloat16),
            pltpu.VMEM(w_query.shape, jnp.bfloat16),
            pltpu.VMEM(w_query.shape, jnp.bfloat16),
            pltpu.SemaphoreType.DMA((3,)),
            pltpu.VMEM((part_rows, n), jnp.float32),
            pltpu.VMEM((part_rows, n), jnp.float32),
            chunks, chunks,
            pltpu.VMEM((heads, 2, full, 4 * HD), jnp.bfloat16),
            pltpu.VMEM((graphs, 2, half, full), jnp.float32),
            pltpu.VMEM(result, jnp.bfloat16),
            pltpu.VMEM(result, jnp.bfloat16),
            pltpu.SemaphoreType.DMA((2,)),
            pltpu.SemaphoreType.DMA((n,)),
            pltpu.SemaphoreType.DMA((n,)),
        ],
        compiler_params=pltpu.CompilerParams(
            vmem_limit_bytes=COLLECT_BYTES, collective_id=1, has_side_effects=True
        ),
        name="collect",
    )(order.reshape(n, 1, part_rows), grads, *in_hbm(w_query, w_key, w_value))


def on_device(
    query, keys_in, values_in, grad_out, w_out, w_query, w_key, w_value, perm, blocks, counts
):
    local_rows, half_width = query.shape
    graphs, nodes = perm.shape
    half_heads = half_width // HD
    part_rows = local_rows // graphs
    n = nodes // part_rows
    graph = lax.axis_index("head") // half_heads
    order = lax.dynamic_index_in_dim(perm, graph, 0, keepdims=False)
    block_row = lax.dynamic_index_in_dim(blocks.transpose(2, 0, 1), graph, 1)
    count_row = lax.dynamic_index_in_dim(counts, graph, 0, keepdims=False)
    by_graph = [
        member.reshape(part_rows, graphs, half_width).transpose(1, 0, 2).reshape(local_rows, half_width)
        for member in (query, keys_in, values_in, grad_out)
    ]
    qg, kv = spreading(order, *by_graph, w_out, n)
    grads = attention(qg, kv, block_row, count_row)
    total = collecting(order, grads, w_query, w_key, w_value, graphs, n)
    return total.transpose(1, 0, 2).reshape(local_rows // 2, -1)


def solution(mesh):
    return jax.shard_map(
        on_device,
        mesh=mesh,
        in_specs=(
            P(("groups", "head"), "tensor"),
            P(("groups", "head"), "tensor"),
            P(("groups", "head"), "tensor"),
            P(("groups", "head"), "tensor"),
            P("tensor", None),
            P(None, "tensor"),
            P(None, "tensor"),
            P(None, "tensor"),
            P("groups", None),
            P("groups", None, None),
            P("groups", None),
        ),
        out_specs=P(("groups", "head", "tensor"), None),
        check_vma=False,
    )
```
